32 devices in a mesh: users: 2 (over x), hist: 8 (over z, y), head: 2 (over core).
Axes of the slice: x: 2, y: 2, z: 4, core: 2. Of those that a mesh axis runs over, the one named last changes fastest.
Arguments:
- candidates: bfloat16 [2048, 512], P(('users', 'hist')), parts along dimension 0, may hold values from -6 to 6
- key_cache: bfloat16 [2, 32768, 512], P(None, ('users', 'hist'), 'head'), parts along dimension 1, may hold values from -6 to 6
- value_cache: bfloat16 [2, 32768, 512], P(None, ('users', 'hist'), 'head'), parts along dimension 1, may hold values from -6 to 6
- w_in: bfloat16 [2, 512, 4, 512], P(None, None, None, 'head'), may hold values from -0.25 to 0.25
- w_out: bfloat16 [2, 512, 512], P(None, 'head'), may hold values from -0.25 to 0.25
- rab_table: float32 [2, 32, 8], P(None, None, 'head'), may hold values from -4 to 4
- hist_len: int32 [16], P(('users', 'hist')), parts along dimension 0, may hold values from 1 to 2048, 8192 in all
- hist_bucket: int32 [32768], P(('users', 'hist')), parts along dimension 0, may hold values from 0 to 31
- visible: int32 [8, 128], P(None, ('users', 'hist')), parts along dimension 1, may hold values 0 or 1
Outputs:
- candidate_out: bfloat16 [2048, 512], P(('users', 'hist')), parts along dimension 0
The draws below stay inside these ranges and needn't reach their ends.
There are 2 independent parts, one for each index of `users`. The reference program is written for one: setup_inputs(seed, part) draws one part's arguments, and reference() takes and returns one part's arrays. A program takes and returns all parts, laid end to end along the dimension named above; an argument that names none is the same for every part. Nothing has to cross between parts.
Inputs may be any that keep to these rules, and one draw needn't show every extreme that they name: `hist_len`: entry s counts the valid events at the start of history shard s; the entries sum to 8192 and the largest is 2048. visible[m, b] is 1 where microbatch m sees history events b * 256 to (b + 1) * 256 - 1.
All inputs are finite; a program needn't handle non-finite values.
Results may differ from the reference program's by a relative error of at most 0.019.
Values may be sent and summed in bfloat16 or wider, within the bound.
A program may use at most 64 MiB of HBM per device.

```python
import math
import jax
import jax.numpy as jnp
import numpy as np
from jax import lax

D = 512
HEADS = 8
DH = 64
LAYERS = 2
NB = 32
BLOCK = 256
MICRO = 8
C = 1024
HIST_DEV = 2048
HIST = 16384
N_HIST = 8


def plant(array, rng, least, high):
    spot = [jax.random.randint(jax.random.fold_in(rng, axis), (), 0, length) for axis, length in enumerate(array.shape)]
    widest = array.shape.index(max(array.shape))
    next_to = spot[:widest] + [(spot[widest] + 1) % array.shape[widest]] + spot[widest + 1:]
    return array.at[tuple(spot)].set(least).at[tuple(next_to)].set(high)


def steps_of(rng, extent, split, low, top_value):
    loudness, own = 1.0, jax.random.fold_in(rng, 6)
    for position, parts in split:
        steps = jnp.exp(jax.random.uniform(jax.random.fold_in(own, position), (parts,), jnp.float32, low / len(split), top_value / len(split)))
        loudness = loudness * jnp.repeat(steps, extent[position] // parts).reshape([-1 if axis == position else 1 for axis in range(len(extent))])
    return loudness


def length_profile(amount, total, bound, lean):
    portions = [(1 << 20) // math.isqrt(grade ** lean) + 1 for grade in range(2, amount + 1)]
    spare, given = total - bound - (amount - 1), [1] * (amount - 1)
    while spare > 0:
        free = [i for i in range(amount - 1) if given[i] < bound]
        pool, budget = sum([portions[i] for i in free]), spare
        for i in free:
            extra = min(bound - given[i], max(1, budget * portions[i] // pool), spare)
            given[i] = given[i] + extra
            spare = spare - extra
    return np.array([bound] + given)


def uneven(own_key, amount, total, bound, lean):
    if amount == 2:
        one = jax.random.randint(own_key, (), max(1, total - bound), min(bound, total - 1) + 1)
        return jnp.stack([one, total - one])
    sizes = jnp.asarray(length_profile(amount, total, bound, lean), jnp.int32)
    twos = (amount - 1) // 2
    source_of, sink = sizes[1:1 + 2 * twos:2], sizes[2:2 + 2 * twos:2]
    slack = jnp.minimum(source_of - 1, bound - sink)
    shifted = jax.random.randint(jax.random.fold_in(own_key, 1), (twos,), 0, 1 << 20) % (slack + 1)
    sizes = sizes.at[1:1 + 2 * twos:2].set(source_of - shifted).at[2:2 + 2 * twos:2].set(sink + shifted)
    return sizes[jax.random.permutation(jax.random.fold_in(own_key, 2), amount)]


def bell_draw(rng, dims, deviation, reach, cuts=(), kind=jnp.bfloat16):
    result = deviation * jax.random.normal(rng, dims, jnp.float32)
    if cuts:
        result = result * steps_of(rng, dims, cuts, -0.22, 0.18)
    return jnp.clip(result, -reach, reach).astype(kind)


def setup_inputs(seed: int = 0, part: int = 0) -> dict:
    key_of = jax.random.split(jax.random.key(seed), 10)
    part_keys = jax.random.split(jax.random.fold_in(key_of[9], part), 10)
    candidates = bell_draw(part_keys[0], (C, D), 1.0, 6.0, ((0, 8),))
    key_cache = bell_draw(part_keys[1], (LAYERS, HIST, HEADS * DH), 1.0, 6.0, ((1, 8), (2, 2)))
    value_cache = bell_draw(part_keys[2], (LAYERS, HIST, HEADS * DH), 1.0, 6.0, ((1, 8), (2, 2)))
    w_in = bell_draw(key_of[3], (LAYERS, D, 4, HEADS * DH), D ** -0.5, 0.25, ((3, 2),))
    w_out = bell_draw(key_of[4], (LAYERS, HEADS * DH, D), (HEADS * DH) ** -0.5, 0.25, ((1, 2),))
    rab_table = bell_draw(key_of[5], (LAYERS, NB, HEADS), 1.0, 4.0, ((2, 2),), jnp.float32)
    hist_len = uneven(part_keys[6], N_HIST, N_HIST * HIST_DEV // 2, HIST_DEV, 2).astype(jnp.int32)
    hist_bucket = plant(jax.random.randint(part_keys[7], (HIST,), 0, NB), jax.random.fold_in(part_keys[7], 1), 0, NB - 1).astype(jnp.int32)
    visible = plant((jax.random.randint(part_keys[8], (MICRO, HIST // BLOCK), 0, 4) < 3).astype(jnp.int32), jax.random.fold_in(part_keys[8], 1), 0, 1)
    return dict(candidates=candidates, key_cache=key_cache, value_cache=value_cache, w_in=w_in, w_out=w_out, rab_table=rab_table, hist_len=hist_len, hist_bucket=hist_bucket, visible=visible)


epsilon = 1e-05

def reference(candidates, key_cache, value_cache, w_in, w_out, rab_table, hist_len, hist_bucket, visible):
    width = HEADS * DH
    factor = DH ** (-0.5)
    stream = candidates.astype(jnp.float32)
    micro_ids = jnp.arange(C, dtype=jnp.int32) // (C // MICRO)
    blocks_shard = HIST_DEV // BLOCK
    for layer_index in range(LAYERS):
        average = lax.optimization_barrier(jnp.mean(stream, axis=-1, keepdims=True))
        centred = stream - average
        variance = lax.optimization_barrier(jnp.mean(centred * centred, axis=-1, keepdims=True))
        normed = (centred * lax.rsqrt(variance + epsilon)).astype(jnp.bfloat16)
        projected = jnp.dot(normed, w_in[layer_index].reshape(D, 4 * width), preferred_element_type=jnp.float32)
        projected = jax.nn.silu(projected).astype(jnp.bfloat16).reshape(C, 4, width)
        queries = projected[:, 0].astype(jnp.float32).reshape(C, HEADS, DH)
        keys_new = projected[:, 1].astype(jnp.float32).reshape(C, HEADS, DH)
        values_new = projected[:, 2].astype(jnp.float32).reshape(C, HEADS, DH)
        gates = projected[:, 3].astype(jnp.float32)
        one_hot = (hist_bucket[:, None] == jnp.arange(NB, dtype=jnp.int32)[None, :]).astype(jnp.float32)
        bias = jnp.dot(one_hot, rab_table[layer_index], precision=lax.Precision.HIGHEST)
        cached_keys = key_cache[layer_index]
        cached_values = value_cache[layer_index]

        def shard_step(summed, shard):
            key_part = lax.dynamic_slice_in_dim(cached_keys, shard * HIST_DEV, HIST_DEV, 0).astype(jnp.float32).reshape(HIST_DEV, HEADS, DH)
            value_part = lax.dynamic_slice_in_dim(cached_values, shard * HIST_DEV, HIST_DEV, 0).astype(jnp.float32).reshape(HIST_DEV, HEADS, DH)
            bias_part = lax.dynamic_slice_in_dim(bias, shard * HIST_DEV, HIST_DEV, 0)
            visible_part = lax.dynamic_slice_in_dim(visible, shard * blocks_shard, blocks_shard, 1)[micro_ids]
            valid = (jnp.arange(HIST_DEV, dtype=jnp.int32) < hist_len[shard]).astype(jnp.float32)
            masking = jnp.repeat(visible_part, BLOCK, axis=1).astype(jnp.float32) * valid[None, :]
            scores = jnp.einsum('chd,khd->hck', queries, key_part) * factor + bias_part.T[:, None, :]
            weights = (jax.nn.silu(scores) * masking[None]).astype(jnp.bfloat16)
            weights = lax.optimization_barrier(weights).astype(jnp.float32)
            partial_value = jnp.einsum('hck,khd->chd', weights, value_part).astype(jnp.bfloat16)
            partial_value = lax.optimization_barrier(partial_value).astype(jnp.float32)
            return (summed + partial_value, None)
        history, _ = lax.scan(shard_step, jnp.zeros((C, HEADS, DH), jnp.float32), jnp.arange(N_HIST, dtype=jnp.int32))
        own_score = jax.nn.silu(lax.optimization_barrier(jnp.sum(queries * keys_new, axis=-1)) * factor)
        attended = (history + own_score[..., None] * values_new).reshape(C, width)
        average = lax.optimization_barrier(jnp.sum(attended, axis=-1, keepdims=True)) / width
        squares = lax.optimization_barrier(jnp.sum(attended * attended, axis=-1, keepdims=True)) / width
        normalized = (attended - average) * lax.rsqrt(squares - average * average + epsilon)
        gated = (normalized * gates).astype(jnp.bfloat16)
        stream = stream + jnp.dot(gated, w_out[layer_index], preferred_element_type=jnp.float32)
    return stream.astype(jnp.bfloat16)
```

```python
import functools

import jax
import jax.numpy as jnp
from jax import lax
from jax.experimental import pallas as pl
from jax.experimental.pallas import tpu as pltpu
from jax.sharding import PartitionSpec as P

DH = 64
BLOCK = 256
LANES = 128
PER = LANES // DH
GROUP_ROWS = 256
KEY_CHUNK = 2048
BIG = 16384.0
MESH = pl.DeviceIdType.MESH

epsilon = 1e-05


def silu(v):
    return v / (1.0 + jnp.exp(-v))


def dot(a, b):
    return jnp.dot(a, b, preferred_element_type=jnp.float32)


def kernel(
    n,
    inner,
    cand_hbm,
    w_hbm,
    key_hbm,
    val_hbm,
    wo_hbm,
    rab_hbm,
    bucket_hbm,
    hlen,
    vis,
    out,
    cand,
    raw,
    wide,
    w_in,
    w_out,
    rab,
    bucket,
    keys,
    vals,
    kaug,
    table,
    events,
    w_other,
    qall,
    qaug,
    part,
    parts_in,
    pair_in,
    merged,
    acc,
    att_send,
    att_in,
    gate_send,
    gate_in,
    load_sem,
    q_send,
    q_recv,
    p_send,
    p_recv,
    y_send,
    y_recv,
    h_send,
    h_recv,
):
    me = lax.axis_index("hist")
    other = 1 - lax.axis_index("head")
    layers, hist_dev, wl = key_hbm.shape
    rows, d = cand.shape
    heads = wl // DH
    parts_w = 4
    pairs = wl // LANES
    nb = rab.shape[2]
    micro, blocks = vis.shape
    total = n * rows
    micro_rows = total // micro
    group_rows = min(GROUP_ROWS, total)
    per_group = group_rows // rows
    groups = n // per_group
    outer = n // inner
    relay = inner == 2 and per_group == inner
    line, side = me // inner, lax.rem(me, inner)
    beside = line * inner + (inner - 1 - side)
    key_chunk = min(KEY_CHUNK, hist_dev)

    load_k = pltpu.make_async_copy(key_hbm, keys, load_sem.at[0])
    load_v = pltpu.make_async_copy(val_hbm, vals, load_sem.at[1])
    load_c = pltpu.make_async_copy(cand_hbm, cand, load_sem.at[2])
    load_w = [
        pltpu.make_async_copy(w_hbm.at[l], raw.at[l], load_sem.at[3 + l]) for l in range(layers)
    ]
    load_o = pltpu.make_async_copy(wo_hbm, w_out, load_sem.at[3 + layers])
    load_r = pltpu.make_async_copy(rab_hbm, rab, load_sem.at[4 + layers])
    load_b = pltpu.make_async_copy(bucket_hbm, bucket, load_sem.at[5 + layers])
    load_c.start()
    load_w[0].start()
    load_b.start()
    load_r.start()
    load_k.start()
    load_o.start()
    load_v.start()
    for copy in load_w[1:]:
        copy.start()

    barrier = pltpu.get_barrier_semaphore()
    for j in range(1, n):
        pl.semaphore_signal(
            barrier, inc=1, device_id={"hist": lax.rem(me + j, n)}, device_id_type=MESH
        )
    pl.semaphore_signal(barrier, inc=1, device_id={"head": other}, device_id_type=MESH)

    def to_head(src, dst, index):
        return pltpu.make_async_remote_copy(
            src_ref=src,
            dst_ref=dst,
            send_sem=h_send.at[index],
            recv_sem=h_recv.at[index],
            device_id={"head": other},
            device_id_type=MESH,
        )

    def unpack_w(l):
        halves = wl // LANES
        step = halves * parts_w
        wide[...] = raw[l].astype(jnp.float32)
        for i in range(parts_w):
            for c in range(halves):
                start = i * wl + c * LANES
                w_in[:, start : start + LANES] = wide[
                    pl.ds(c * parts_w + i, d, stride=step), :
                ].astype(jnp.bfloat16)

    def row_of(s):
        return pl.ds(pl.multiple_of(s * rows, rows), rows)

    def q_copy(l, s, owner):
        return pltpu.make_async_remote_copy(
            src_ref=qall.at[l, row_of(owner)],
            dst_ref=qall.at[l, row_of(owner)],
            send_sem=q_send.at[l, s],
            recv_sem=q_recv.at[l, owner],
            device_id={"hist": s},
            device_id_type=MESH,
        )

    def p_copy(l, s, owner):
        return pltpu.make_async_remote_copy(
            src_ref=part.at[l, row_of(s)],
            dst_ref=parts_in.at[l, owner],
            send_sem=p_send.at[l, s],
            recv_sem=p_recv.at[l, owner],
            device_id={"hist": s},
            device_id_type=MESH,
        )

    def y_copy(l, z):
        return pltpu.make_async_remote_copy(
            src_ref=part.at[l, row_of(z * inner + (inner - 1 - side))],
            dst_ref=pair_in.at[l, z],
            send_sem=y_send.at[l, z],
            recv_sem=y_recv.at[l, z],
            device_id={"hist": beside},
            device_id_type=MESH,
        )

    def m_copy(l, z, owner):
        return pltpu.make_async_remote_copy(
            src_ref=merged.at[l, z],
            dst_ref=parts_in.at[l, owner],
            send_sem=p_send.at[l, z],
            recv_sem=p_recv.at[l, owner],
            device_id={"hist": z * inner + side},
            device_id_type=MESH,
        )

    def merge(l, z):
        y_copy(l, z).wait_recv()
        both = part[l, row_of(z * inner + side), :].astype(jnp.float32)
        both = both + pair_in[l, z].astype(jnp.float32)
        merged[l, z] = both.astype(jnp.bfloat16)
        m_copy(l, z, line).start()

    def build_keys():
        lane = lax.broadcasted_iota(jnp.int32, (LANES, LANES), 1)
        lane8 = lax.broadcasted_iota(jnp.int32, (blocks, LANES), 1)
        row8 = lax.broadcasted_iota(jnp.int32, (blocks, LANES), 0)
        base_of = (DH, 0)
        seen = []
        gone = []
        for base in base_of:
            held = jnp.zeros((blocks, LANES), jnp.float32)
            for m in range(micro):
                column = jnp.zeros((blocks, LANES), jnp.float32)
                for b in range(blocks):
                    value = (vis[m, b] - 1).astype(jnp.float32) * BIG
                    column = jnp.where(row8 == b, value, column)
                held = jnp.where(lane8 == base + 2 + m, column, held)
            seen.append(held)
            is_micro = (lane8 >= base + 2) & (lane8 < base + 2 + micro)
            gone.append(jnp.where(is_micro & (row8 == 0), -BIG, 0.0))
        for l in range(layers):
            flat = jnp.concatenate([rab[l], jnp.zeros((heads, LANES - nb), jnp.float32)], axis=1)
            flat = jnp.concatenate([flat, jnp.zeros((8 - heads, LANES), jnp.float32)], axis=0)
            upright = flat.T
            for h in range(heads):
                base = base_of[h % PER]
                half = upright[:nb, h : h + 1] * 0.5
                high = half.astype(jnp.bfloat16).astype(jnp.float32)
                low = half - high
                lane_nb = lane[:nb]
                bias = jnp.where(lane_nb == base, high, jnp.where(lane_nb == base + 1, low, 0.0))
                fill = jnp.zeros((LANES - nb - 2 * blocks, LANES), jnp.float32)
                whole = jnp.concatenate([bias, seen[h % PER], gone[h % PER], fill], axis=0)
                start = (l * heads + h) * LANES
                table[:, start : start + LANES] = whole.astype(jnp.bfloat16)

        row = lax.broadcasted_iota(jnp.int32, (LANES, key_chunk), 0)
        spot = lax.broadcasted_iota(jnp.int32, (LANES, key_chunk), 1)
        lane_k = lax.broadcasted_iota(jnp.int32, (key_chunk, LANES), 1)
        length = hlen[0]
        for c in range(hist_dev // key_chunk):
            span = slice(c * key_chunk, (c + 1) * key_chunk)
            place = spot + c * key_chunk
            here = (
                (row == bucket[:, span])
                | (row == nb + place // BLOCK)
                | ((row == nb + blocks) & (place >= length))
            )
            events[span, :] = jnp.where(here, 1.0, 0.0).T.astype(jnp.bfloat16)
        load_k.wait()

        def chunk(c, carry):
            span = pl.ds(pl.multiple_of(c * key_chunk, key_chunk), key_chunk)
            spread = events[span, :]
            for l in range(layers):
                for h in range(heads):
                    start = (l * heads + h) * LANES
                    extra = dot(spread, table[:, start : start + LANES])
                    p = h // PER
                    tile = keys[l, span, p * LANES : (p + 1) * LANES].astype(jnp.float32)
                    mine = (lane_k < DH) if h % PER == 0 else (lane_k >= DH)
                    kaug[l, h, span, :] = jnp.where(mine, tile, extra).astype(jnp.bfloat16)
            return carry

        lax.fori_loop(0, hist_dev // key_chunk, chunk, 0)

    lane_q = lax.broadcasted_iota(jnp.int32, (group_rows, LANES), 1)
    row_q = lax.broadcasted_iota(jnp.int32, (group_rows, LANES), 0)
    lane_a = lax.broadcasted_iota(jnp.int32, (group_rows, LANES), 1)

    def attend(l, g):
        span = pl.ds(pl.multiple_of(g * group_rows, group_rows), group_rows)
        which = (row_q + g * group_rows) // micro_rows
        for h in range(heads):
            p = h // PER
            base = DH if h % PER == 0 else 0
            tile = qall[l, span, p * LANES : (p + 1) * LANES].astype(jnp.float32)
            ones = (lane_q == base) | (lane_q == base + 1) | (lane_q == base + 2 + which)
            mine = (lane_q < DH) if h % PER == 0 else (lane_q >= DH)
            qaug[h] = jnp.where(mine, tile, jnp.where(ones, 1.0, 0.0)).astype(jnp.bfloat16)
        acc[...] = jnp.zeros_like(acc)

        def chunk(c, carry):
            keys_at = pl.ds(pl.multiple_of(c * key_chunk, key_chunk), key_chunk)
            for p in range(pairs):
                value = vals[l, keys_at, p * LANES : (p + 1) * LANES]
                found = []
                for e in range(PER):
                    h = p * PER + e
                    y = lax.dot_general(
                        qaug[h],
                        kaug[l, h, keys_at, :],
                        (((1,), (1,)), ((), ())),
                        preferred_element_type=jnp.float32,
                    ).astype(jnp.bfloat16)
                    weight = y * (jnp.tanh(y) + 1.0)
                    found.append(dot(weight, value))
                acc[:, p * LANES : (p + 1) * LANES] += jnp.where(lane_a < DH, found[0], found[1])
            return carry

        lax.fori_loop(0, hist_dev // key_chunk, chunk, 0)
        part[l, span, :] = acc[...].astype(jnp.bfloat16)

    block_row = lax.broadcasted_iota(jnp.int32, (wl, wl), 0) // DH
    block_col = lax.broadcasted_iota(jnp.int32, (wl, wl), 1) // DH
    same_head = jnp.where(block_row == block_col, 1.0, 0.0).astype(jnp.bfloat16)

    load_c.wait()
    stream = cand[...].astype(jnp.float32)
    for l in range(layers):
        load_w[l].wait()
        unpack_w(l)
        average = jnp.mean(stream, axis=-1, keepdims=True)
        centred = stream - average
        variance = jnp.mean(centred * centred, axis=-1, keepdims=True)
        normed = (centred * lax.rsqrt(variance + epsilon)).astype(jnp.bfloat16)

        def project(i):
            return silu(dot(normed, w_in[:, i * wl : (i + 1) * wl])).astype(jnp.bfloat16)

        queries = project(0).astype(jnp.float32)
        qall[l, row_of(me), :] = (queries * (0.5 * DH**-0.5)).astype(jnp.bfloat16)
        if l == 0:
            pl.semaphore_wait(barrier, n)
        if relay:
            for j in range(1, outer):
                z = lax.rem(line + outer - j, outer)
                q_copy(l, z * inner + side, me).start()
                q_copy(l, z * inner + (inner - 1 - side), me).start()
            q_copy(l, beside, me).start()
        else:
            for j in range(1, n):
                q_copy(l, lax.rem(me + j, n), me).start()
        keys_new = project(1).astype(jnp.float32)
        values_new = project(2).astype(jnp.float32)
        gates = project(3)
        gate_send[l] = gates
        gate_copy = to_head(gate_send.at[l], gate_in.at[l], 2 * l)
        gate_copy.start()
        if l == 0:
            load_o.wait()
            w_copy = to_head(w_out, w_other, 2 * layers)
            w_copy.start()
        product = queries * keys_new
        high = product.astype(jnp.bfloat16)
        low = (product - high.astype(jnp.float32)).astype(jnp.bfloat16)
        own_score = dot(high, same_head) + dot(low, same_head)
        own = silu(own_score * (DH**-0.5)) * values_new
        if l == 0:
            load_r.wait()
            load_b.wait()
            build_keys()
            load_v.wait()

        def group(t, carry):
            g = lax.rem(me // per_group + t, groups)
            for i in range(per_group):
                s = g * per_group + i

                @pl.when(s != me)
                def _():
                    q_copy(l, s, s).wait_recv()

            attend(l, g)
            for i in range(per_group):
                s = g * per_group + i

                @pl.when(s != me)
                def _():
                    p_copy(l, s, me).start()

            return carry

        def relayed(t, carry):
            z = lax.rem(line + t + 1, outer)
            for i in range(inner):
                s = z * inner + i

                @pl.when(s != me)
                def _():
                    q_copy(l, s, s).wait_recv()

            attend(l, z)
            y_copy(l, z).start()

            @pl.when(t > 0)
            def _():
                merge(l, lax.rem(line + t, outer))

            return carry

        if relay:
            lax.fori_loop(0, outer, relayed, 0)
            y_copy(l, line).wait_recv()
            history = part[l, row_of(me), :].astype(jnp.float32)
            history = history + pair_in[l, line].astype(jnp.float32)
            for j in range(1, outer):
                z = lax.rem(line + outer - j, outer)
                m_copy(l, z, z).wait_recv()
                history = history + parts_in[l, z].astype(jnp.float32)
        else:
            lax.fori_loop(0, groups, group, 0)
            history = part[l, row_of(me), :].astype(jnp.float32)
            for j in range(1, n):
                s = lax.rem(me + j, n)
                p_copy(l, s, s).wait_recv()
                history = history + parts_in[l, s].astype(jnp.float32)
        attended = history + own
        att_send[l] = attended
        att_copy = to_head(att_send.at[l], att_in.at[l], 2 * l + 1)
        att_copy.start()
        if l == 0:
            w_copy.wait_recv()
        gate_copy.wait_recv()
        att_copy.wait_recv()
        theirs = att_in[l]
        width = 2 * wl
        mean = (
            jnp.sum(attended, axis=-1, keepdims=True) + jnp.sum(theirs, axis=-1, keepdims=True)
        ) / width
        square = (
            jnp.sum(attended * attended, axis=-1, keepdims=True)
            + jnp.sum(theirs * theirs, axis=-1, keepdims=True)
        ) / width
        rstd = lax.rsqrt(square - mean * mean + epsilon)
        gated = ((attended - mean) * rstd * gates.astype(jnp.float32)).astype(jnp.bfloat16)
        gated_other = ((theirs - mean) * rstd * gate_in[l].astype(jnp.float32)).astype(
            jnp.bfloat16
        )
        stream = stream + (dot(gated, w_out[l]) + dot(gated_other, w_other[l]))
        gate_copy.wait_send()
        att_copy.wait_send()
        if l == 0:
            w_copy.wait_send()
        if relay:
            for j in range(1, n):
                q_copy(l, lax.rem(me + j, n), me).wait_send()
            y_copy(l, line).wait_send()
            for j in range(1, outer):
                z = lax.rem(line + j, outer)
                y_copy(l, z).wait_send()
                m_copy(l, z, line).wait_send()
        else:
            for j in range(1, n):
                s = lax.rem(me + j, n)
                q_copy(l, s, me).wait_send()
                p_copy(l, s, me).wait_send()
    out[...] = stream.astype(out.dtype)


def shards(
    n, inner, candidates, key_cache, value_cache, w_in, w_out, rab_table, hist_len, hist_bucket, visible
):
    layers, hist_dev, wl = key_cache.shape
    rows, d = candidates.shape
    heads = wl // DH
    total = n * rows
    group_rows = min(GROUP_ROWS, total)
    bf16, f32 = jnp.bfloat16, jnp.float32
    vmem = pl.BlockSpec(memory_space=pltpu.VMEM)
    smem = pl.BlockSpec(memory_space=pltpu.SMEM)
    hbm = pl.BlockSpec(memory_space=pltpu.HBM)
    dma = pltpu.SemaphoreType.DMA
    return pl.pallas_call(
        functools.partial(kernel, n, inner),
        out_shape=jax.ShapeDtypeStruct((rows, d), bf16),
        in_specs=[hbm, hbm, hbm, hbm, hbm, hbm, hbm, smem, smem],
        out_specs=vmem,
        scratch_shapes=[
            pltpu.VMEM((rows, d), bf16),
            pltpu.VMEM((layers, d * 4 * wl // LANES, LANES), bf16),
            pltpu.VMEM((d * 4 * wl // LANES, LANES), f32),
            pltpu.VMEM((d, 4 * wl), bf16),
            pltpu.VMEM(w_out.shape, bf16),
            pltpu.VMEM((layers, heads, rab_table.shape[1]), f32),
            pltpu.VMEM((1, hist_dev), jnp.int32),
            pltpu.VMEM((layers, hist_dev, wl), bf16),
            pltpu.VMEM((layers, hist_dev, wl), bf16),
            pltpu.VMEM((layers, heads, hist_dev, LANES), bf16),
            pltpu.VMEM((LANES, layers * heads * LANES), bf16),
            pltpu.VMEM((hist_dev, LANES), bf16),
            pltpu.VMEM(w_out.shape, bf16),
            pltpu.VMEM((layers, total, wl), bf16),
            pltpu.VMEM((heads, group_rows, LANES), bf16),
            pltpu.VMEM((layers, total, wl), bf16),
            pltpu.VMEM((layers, n, rows, wl), bf16),
            pltpu.VMEM((layers, n // inner, rows, wl), bf16),
            pltpu.VMEM((layers, n // inner, rows, wl), bf16),
            pltpu.VMEM((group_rows, wl), f32),
            pltpu.VMEM((layers, rows, wl), f32),
            pltpu.VMEM((layers, rows, wl), f32),
            pltpu.VMEM((layers, rows, wl), bf16),
            pltpu.VMEM((layers, rows, wl), bf16),
            dma((6 + layers,)),
            dma((layers, n)),
            dma((layers, n)),
            dma((layers, n)),
            dma((layers, n)),
            dma((layers, n)),
            dma((layers, n)),
            dma((2 * layers + 1,)),
            dma((2 * layers + 1,)),
        ],
        compiler_params=pltpu.CompilerParams(
            collective_id=0, has_side_effects=True, vmem_limit_bytes=60 * 1024 * 1024
        ),
    )(
        candidates,
        w_in.reshape(layers, d, 4, wl // LANES, LANES)
        .transpose(0, 1, 3, 2, 4)
        .reshape(layers, d * 4 * wl // LANES, LANES),
        key_cache,
        value_cache,
        w_out,
        rab_table.transpose(0, 2, 1),
        hist_bucket.reshape(1, hist_dev),
        hist_len,
        visible,
    )


def inner_of(mesh):
    n = mesh.shape["hist"]
    if n % 2 or n < 4:
        return 1
    index = [slice(None) if name == "hist" else 0 for name in mesh.axis_names]
    spots = [getattr(device, "coords", None) for device in mesh.devices[tuple(index)][:3]]
    if any(spot is None for spot in spots):
        return 1
    apart = [sum(abs(a - b) for a, b in zip(spots[0], spot)) for spot in spots[1:]]
    return 2 if apart == [1, 1] else 1


def solution(mesh):
    placed = (
        P(("users", "hist"), None),
        P(None, ("users", "hist"), "head"),
        P(None, ("users", "hist"), "head"),
        P(None, None, None, "head"),
        P(None, "head", None),
        P(None, None, "head"),
        P(("users", "hist")),
        P(("users", "hist")),
        P(None, ("users", "hist")),
    )
    return jax.shard_map(
        functools.partial(shards, mesh.shape["hist"], inner_of(mesh)),
        mesh=mesh,
        in_specs=placed,
        out_specs=P(("users", "hist"), None),
        check_vma=False,
    )
```

```python
import functools

import jax
import jax.numpy as jnp
from jax import lax
from jax.experimental import pallas as pl
from jax.experimental.pallas import tpu as pltpu
from jax.sharding import PartitionSpec as P

DH = 64
BLOCK = 256
LANES = 128
PER = LANES // DH
GROUP_ROWS = 256
KEY_CHUNK = 2048
BIG = 16384.0
MESH = pl.DeviceIdType.MESH
HALVES = 2
RELAY = ((True, True), (True, True))
RELAYS = sum(on << (2 * k + f) for k, two in enumerate(RELAY) for f, on in enumerate(two))
SENDS = ((3, 0), (3, 1), (0, 1), (1, 0), (1, 1), (2, 0), (2, 1))
GATHER = ((3, 0), (3, 1), (1, 0), (1, 1), (2, 0), (2, 1), (0, 1))
ORDER = ((1, 3, 0, 2, 1, 3, 2, 0), (1, 3, 0, 2, 1, 3, 2, 0))
ORDERS = [sum(dz << (2 * t) for t, dz in enumerate(order)) for order in ORDER]
SUM_B = 0

epsilon = 1e-05


def silu(v):
    return v / (1.0 + jnp.exp(-v))


def dot(a, b):
    return jnp.dot(a, b, preferred_element_type=jnp.float32)


def kernel(
    n,
    cand_hbm,
    w_hbm,
    key_hbm,
    val_hbm,
    wo_hbm,
    rab_hbm,
    bucket_hbm,
    hlen,
    vis,
    out,
    cand,
    raw,
    wide,
    w_in,
    w_out,
    rab,
    bucket,
    keys,
    vals,
    kaug,
    table,
    events,
    w_other,
    qall,
    qaug,
    part,
    parts_in,
    acc,
    att_send,
    att_in,
    gate_send,
    gate_in,
    load_sem,
    q_send,
    q_recv,
    p_send,
    p_recv,
    h_send,
    h_recv,
):
    me = lax.axis_index("hist")
    other = 1 - lax.axis_index("head")
    layers, hist_dev, wl = key_hbm.shape
    rows, d = cand.shape
    heads = wl // DH
    parts_w = 4
    pairs = wl // LANES
    nb = rab.shape[2]
    micro, blocks = vis.shape
    total = n * rows
    micro_rows = total // micro
    group_rows = min(GROUP_ROWS, total)
    per_group = group_rows // rows
    groups = n // per_group
    key_chunk = min(KEY_CHUNK, hist_dev)

    load_k = pltpu.make_async_copy(key_hbm, keys, load_sem.at[0])
    load_v = pltpu.make_async_copy(val_hbm, vals, load_sem.at[1])
    load_c = pltpu.make_async_copy(cand_hbm, cand, load_sem.at[2])
    load_w = [
        pltpu.make_async_copy(w_hbm.at[l], raw.at[l], load_sem.at[3 + l]) for l in range(layers)
    ]
    load_o = pltpu.make_async_copy(wo_hbm, w_out, load_sem.at[3 + layers])
    load_r = pltpu.make_async_copy(rab_hbm, rab, load_sem.at[4 + layers])
    load_b = pltpu.make_async_copy(bucket_hbm, bucket, load_sem.at[5 + layers])
    load_c.start()
    load_w[0].start()
    load_b.start()
    load_r.start()
    load_k.start()
    load_o.start()
    load_v.start()
    for copy in load_w[1:]:
        copy.start()

    barrier = pltpu.get_barrier_semaphore()
    for j in range(1, n):
        pl.semaphore_signal(
            barrier, inc=1, device_id={"hist": lax.rem(me + j, n)}, device_id_type=MESH
        )
    pl.semaphore_signal(barrier, inc=1, device_id={"head": other}, device_id_type=MESH)

    def to_head(src, dst, index):
        return pltpu.make_async_remote_copy(
            src_ref=src,
            dst_ref=dst,
            send_sem=h_send.at[index],
            recv_sem=h_recv.at[index],
            device_id={"head": other},
            device_id_type=MESH,
        )

    def unpack_w(l):
        halves = wl // LANES
        step = halves * parts_w
        wide[...] = raw[l].astype(jnp.float32)
        for i in range(parts_w):
            for c in range(halves):
                start = i * wl + c * LANES
                w_in[:, start : start + LANES] = wide[
                    pl.ds(c * parts_w + i, d, stride=step), :
                ].astype(jnp.bfloat16)

    def row_of(s):
        return pl.ds(pl.multiple_of(s * rows, rows), rows)

    def q_copy(l, s, owner):
        return pltpu.make_async_remote_copy(
            src_ref=qall.at[l, row_of(owner)],
            dst_ref=qall.at[l, row_of(owner)],
            send_sem=q_send.at[l, s],
            recv_sem=q_recv.at[l, owner],
            device_id={"hist": s},
            device_id_type=MESH,
        )

    def p_copy(l, s, owner):
        return pltpu.make_async_remote_copy(
            src_ref=part.at[l, row_of(s)],
            dst_ref=parts_in.at[l, owner],
            send_sem=p_send.at[l, s],
            recv_sem=p_recv.at[l, owner],
            device_id={"hist": s},
            device_id_type=MESH,
        )

    def build_keys():
        lane = lax.broadcasted_iota(jnp.int32, (LANES, LANES), 1)
        lane8 = lax.broadcasted_iota(jnp.int32, (blocks, LANES), 1)
        row8 = lax.broadcasted_iota(jnp.int32, (blocks, LANES), 0)
        base_of = (DH, 0)
        seen = []
        gone = []
        for base in base_of:
            held = jnp.zeros((blocks, LANES), jnp.float32)
            for m in range(micro):
                column = jnp.zeros((blocks, LANES), jnp.float32)
                for b in range(blocks):
                    value = (vis[m, b] - 1).astype(jnp.float32) * BIG
                    column = jnp.where(row8 == b, value, column)
                held = jnp.where(lane8 == base + 2 + m, column, held)
            seen.append(held)
            is_micro = (lane8 >= base + 2) & (lane8 < base + 2 + micro)
            gone.append(jnp.where(is_micro & (row8 == 0), -BIG, 0.0))
        for l in range(layers):
            flat = jnp.concatenate([rab[l], jnp.zeros((heads, LANES - nb), jnp.float32)], axis=1)
            flat = jnp.concatenate([flat, jnp.zeros((8 - heads, LANES), jnp.float32)], axis=0)
            upright = flat.T
            for h in range(heads):
                base = base_of[h % PER]
                half = upright[:nb, h : h + 1] * 0.5
                high = half.astype(jnp.bfloat16).astype(jnp.float32)
                low = half - high
                lane_nb = lane[:nb]
                bias = jnp.where(lane_nb == base, high, jnp.where(lane_nb == base + 1, low, 0.0))
                fill = jnp.zeros((LANES - nb - 2 * blocks, LANES), jnp.float32)
                whole = jnp.concatenate([bias, seen[h % PER], gone[h % PER], fill], axis=0)
                start = (l * heads + h) * LANES
                table[:, start : start + LANES] = whole.astype(jnp.bfloat16)

        row = lax.broadcasted_iota(jnp.int32, (LANES, key_chunk), 0)
        spot = lax.broadcasted_iota(jnp.int32, (LANES, key_chunk), 1)
        lane_k = lax.broadcasted_iota(jnp.int32, (key_chunk, LANES), 1)
        length = hlen[0]
        for c in range(hist_dev // key_chunk):
            span = slice(c * key_chunk, (c + 1) * key_chunk)
            place = spot + c * key_chunk
            here = (
                (row == bucket[:, span])
                | (row == nb + place // BLOCK)
                | ((row == nb + blocks) & (place >= length))
            )
            events[span, :] = jnp.where(here, 1.0, 0.0).T.astype(jnp.bfloat16)
        load_k.wait()

        def chunk(c, carry):
            span = pl.ds(pl.multiple_of(c * key_chunk, key_chunk), key_chunk)
            spread = events[span, :]
            for l in range(layers):
                for h in range(heads):
                    start = (l * heads + h) * LANES
                    extra = dot(spread, table[:, start : start + LANES])
                    p = h // PER
                    tile = keys[l, span, p * LANES : (p + 1) * LANES].astype(jnp.float32)
                    mine = (lane_k < DH) if h % PER == 0 else (lane_k >= DH)
                    kaug[l, h, span, :] = jnp.where(mine, tile, extra).astype(jnp.bfloat16)
            return carry

        lax.fori_loop(0, hist_dev // key_chunk, chunk, 0)

    lane_q = lax.broadcasted_iota(jnp.int32, (group_rows, LANES), 1)
    row_q = lax.broadcasted_iota(jnp.int32, (group_rows, LANES), 0)
    lane_a = lax.broadcasted_iota(jnp.int32, (group_rows, LANES), 1)

    def attend(l, g):
        span = pl.ds(pl.multiple_of(g * group_rows, group_rows), group_rows)
        which = (row_q + g * group_rows) // micro_rows
        for h in range(heads):
            p = h // PER
            base = DH if h % PER == 0 else 0
            tile = qall[l, span, p * LANES : (p + 1) * LANES].astype(jnp.float32)
            ones = (lane_q == base) | (lane_q == base + 1) | (lane_q == base + 2 + which)
            mine = (lane_q < DH) if h % PER == 0 else (lane_q >= DH)
            qaug[h] = jnp.where(mine, tile, jnp.where(ones, 1.0, 0.0)).astype(jnp.bfloat16)
        acc[...] = jnp.zeros_like(acc)

        def chunk(c, carry):
            keys_at = pl.ds(pl.multiple_of(c * key_chunk, key_chunk), key_chunk)
            for p in range(pairs):
                value = vals[l, keys_at, p * LANES : (p + 1) * LANES]
                found = []
                for e in range(PER):
                    h = p * PER + e
                    y = lax.dot_general(
                        qaug[h],
                        kaug[l, h, keys_at, :],
                        (((1,), (1,)), ((), ())),
                        preferred_element_type=jnp.float32,
                    ).astype(jnp.bfloat16)
                    weight = y * (jnp.tanh(y) + 1.0)
                    found.append(dot(weight, value))
                acc[:, p * LANES : (p + 1) * LANES] += jnp.where(lane_a < DH, found[0], found[1])
            return carry

        lax.fori_loop(0, hist_dev // key_chunk, chunk, 0)
        part[l, span, :] = acc[...].astype(jnp.bfloat16)

    block_row = lax.broadcasted_iota(jnp.int32, (wl, wl), 0) // DH
    block_col = lax.broadcasted_iota(jnp.int32, (wl, wl), 1) // DH
    same_head = jnp.where(block_row == block_col, 1.0, 0.0).astype(jnp.bfloat16)

    load_c.wait()
    stream = cand[...].astype(jnp.float32)
    for l in range(layers):
        load_w[l].wait()
        unpack_w(l)
        average = jnp.mean(stream, axis=-1, keepdims=True)
        centred = stream - average
        variance = jnp.mean(centred * centred, axis=-1, keepdims=True)
        normed = (centred * lax.rsqrt(variance + epsilon)).astype(jnp.bfloat16)

        def project(i):
            return silu(dot(normed, w_in[:, i * wl : (i + 1) * wl])).astype(jnp.bfloat16)

        queries = project(0).astype(jnp.float32)
        qall[l, row_of(me), :] = (queries * (0.5 * DH**-0.5)).astype(jnp.bfloat16)
        if l == 0:
            pl.semaphore_wait(barrier, n)
        for j in range(1, n):
            q_copy(l, lax.rem(me + j, n), me).start()
        keys_new = project(1).astype(jnp.float32)
        values_new = project(2).astype(jnp.float32)
        gates = project(3)
        gate_send[l] = gates
        gate_copy = to_head(gate_send.at[l], gate_in.at[l], 2 * l)
        gate_copy.start()
        if l == 0:
            load_o.wait()
            w_copy = to_head(w_out, w_other, 2 * layers)
            w_copy.start()
        product = queries * keys_new
        high = product.astype(jnp.bfloat16)
        low = (product - high.astype(jnp.float32)).astype(jnp.bfloat16)
        own_score = dot(high, same_head) + dot(low, same_head)
        own = silu(own_score * (DH**-0.5)) * values_new
        if l == 0:
            load_r.wait()
            load_b.wait()
            build_keys()
            load_v.wait()

        def group(t, carry):
            g = lax.rem(me // per_group + t, groups)
            for i in range(per_group):
                s = g * per_group + i

                @pl.when(s != me)
                def _():
                    q_copy(l, s, s).wait_recv()

            attend(l, g)
            for i in range(per_group):
                s = g * per_group + i

                @pl.when(s != me)
                def _():
                    p_copy(l, s, me).start()

            return carry

        lax.fori_loop(0, groups, group, 0)
        history = part[l, row_of(me), :].astype(jnp.float32)
        for j in range(1, n):
            s = lax.rem(me + j, n)
            p_copy(l, s, s).wait_recv()
            history = history + parts_in[l, s].astype(jnp.float32)
        attended = history + own
        att_send[l] = attended
        att_copy = to_head(att_send.at[l], att_in.at[l], 2 * l + 1)
        att_copy.start()
        if l == 0:
            w_copy.wait_recv()
        gate_copy.wait_recv()
        att_copy.wait_recv()
        theirs = att_in[l]
        width = 2 * wl
        mean = (
            jnp.sum(attended, axis=-1, keepdims=True) + jnp.sum(theirs, axis=-1, keepdims=True)
        ) / width
        square = (
            jnp.sum(attended * attended, axis=-1, keepdims=True)
            + jnp.sum(theirs * theirs, axis=-1, keepdims=True)
        ) / width
        rstd = lax.rsqrt(square - mean * mean + epsilon)
        gated = ((attended - mean) * rstd * gates.astype(jnp.float32)).astype(jnp.bfloat16)
        gated_other = ((theirs - mean) * rstd * gate_in[l].astype(jnp.float32)).astype(
            jnp.bfloat16
        )
        stream = stream + (dot(gated, w_out[l]) + dot(gated_other, w_other[l]))
        gate_copy.wait_send()
        att_copy.wait_send()
        if l == 0:
            w_copy.wait_send()
        for j in range(1, n):
            s = lax.rem(me + j, n)
            q_copy(l, s, me).wait_send()
            p_copy(l, s, me).wait_send()
    out[...] = stream.astype(out.dtype)


def shards(
    n, candidates, key_cache, value_cache, w_in, w_out, rab_table, hist_len, hist_bucket, visible
):
    layers, hist_dev, wl = key_cache.shape
    rows, d = candidates.shape
    heads = wl // DH
    total = n * rows
    group_rows = min(GROUP_ROWS, total)
    bf16, f32 = jnp.bfloat16, jnp.float32
    vmem = pl.BlockSpec(memory_space=pltpu.VMEM)
    smem = pl.BlockSpec(memory_space=pltpu.SMEM)
    hbm = pl.BlockSpec(memory_space=pltpu.HBM)
    dma = pltpu.SemaphoreType.DMA
    return pl.pallas_call(
        functools.partial(kernel, n),
        out_shape=jax.ShapeDtypeStruct((rows, d), bf16),
        in_specs=[hbm, hbm, hbm, hbm, hbm, hbm, hbm, smem, smem],
        out_specs=vmem,
        scratch_shapes=[
            pltpu.VMEM((rows, d), bf16),
            pltpu.VMEM((layers, d * 4 * wl // LANES, LANES), bf16),
            pltpu.VMEM((d * 4 * wl // LANES, LANES), f32),
            pltpu.VMEM((d, 4 * wl), bf16),
            pltpu.VMEM(w_out.shape, bf16),
            pltpu.VMEM((layers, heads, rab_table.shape[1]), f32),
            pltpu.VMEM((1, hist_dev), jnp.int32),
            pltpu.VMEM((layers, hist_dev, wl), bf16),
            pltpu.VMEM((layers, hist_dev, wl), bf16),
            pltpu.VMEM((layers, heads, hist_dev, LANES), bf16),
            pltpu.VMEM((LANES, layers * heads * LANES), bf16),
            pltpu.VMEM((hist_dev, LANES), bf16),
            pltpu.VMEM(w_out.shape, bf16),
            pltpu.VMEM((layers, total, wl), bf16),
            pltpu.VMEM((heads, group_rows, LANES), bf16),
            pltpu.VMEM((layers, total, wl), bf16),
            pltpu.VMEM((layers, n, rows, wl), bf16),
            pltpu.VMEM((group_rows, wl), f32),
            pltpu.VMEM((layers, rows, wl), f32),
            pltpu.VMEM((layers, rows, wl), f32),
            pltpu.VMEM((layers, rows, wl), bf16),
            pltpu.VMEM((layers, rows, wl), bf16),
            dma((6 + layers,)),
            dma((layers, n)),
            dma((layers, n)),
            dma((layers, n)),
            dma((layers, n)),
            dma((2 * layers + 1,)),
            dma((2 * layers + 1,)),
        ],
        compiler_params=pltpu.CompilerParams(
            collective_id=0, has_side_effects=True, vmem_limit_bytes=60 * 1024 * 1024
        ),
    )(
        candidates,
        w_in.reshape(layers, d, 4, wl // LANES, LANES)
        .transpose(0, 1, 3, 2, 4)
        .reshape(layers, d * 4 * wl // LANES, LANES),
        key_cache,
        value_cache,
        w_out,
        rab_table.transpose(0, 2, 1),
        hist_bucket.reshape(1, hist_dev),
        hist_len,
        visible,
    )


def pair_kernel(
    n,
    cand_hbm,
    w_hbm,
    key_hbm,
    val_hbm,
    wo_hbm,
    rab_hbm,
    bucket_hbm,
    hlen,
    vis,
    out,
    cand,
    raw,
    wide,
    w_in,
    w_out,
    rab,
    bucket,
    keys,
    vals,
    kaug,
    table,
    events,
    w_other,
    qall,
    qaug,
    part,
    parts_in,
    stream,
    normed,
    q_own,
    own,
    att_send,
    att_in,
    gate_send,
    gate_in,
    load_sem,
    q_send,
    q_recv,
    p_send,
    p_recv,
    a_send,
    a_recv,
    g_send,
    g_recv,
    w_send,
    w_recv,
):
    me = lax.axis_index("hist")
    other = 1 - lax.axis_index("head")
    layers, hist_dev, wl = key_hbm.shape
    rows, d = cand.shape
    heads = wl // DH
    pairs = wl // LANES
    nb = rab.shape[2]
    micro, blocks = vis.shape
    micro_rows = n * rows // micro
    half = rows // HALVES
    pair = 2 * half
    outer = n // 2
    calls = HALVES * outer
    line, side = me // 2, lax.rem(me, 2)
    beside = line * 2 + 1 - side

    load_c = pltpu.make_async_copy(cand_hbm, cand, load_sem.at[0])
    load_w = [
        pltpu.make_async_copy(w_hbm.at[l], raw.at[l], load_sem.at[6 + l]) for l in range(layers)
    ]
    load_k = pltpu.make_async_copy(key_hbm, keys, load_sem.at[1])
    load_v = pltpu.make_async_copy(val_hbm, vals, load_sem.at[2])
    load_o = pltpu.make_async_copy(wo_hbm, w_out, load_sem.at[3])
    load_r = pltpu.make_async_copy(rab_hbm, rab, load_sem.at[4])
    load_b = pltpu.make_async_copy(bucket_hbm, bucket, load_sem.at[5])
    load_c.start()
    load_w[0].start()

    barrier = pltpu.get_barrier_semaphore()
    for j in range(1, n):
        pl.semaphore_signal(
            barrier, inc=1, device_id={"hist": lax.rem(me + j, n)}, device_id_type=MESH
        )
    pl.semaphore_signal(barrier, inc=1, device_id={"head": other}, device_id_type=MESH)

    load_b.start()
    load_r.start()
    load_k.start()
    load_o.start()
    load_v.start()
    for copy in load_w[1:]:
        copy.start()

    def to_head(src, dst, send, recv):
        return pltpu.make_async_remote_copy(
            src_ref=src,
            dst_ref=dst,
            send_sem=send,
            recv_sem=recv,
            device_id={"head": other},
            device_id_type=MESH,
        )

    w_copy = to_head(w_out, w_other, w_send, w_recv)

    def att_copy(l, f):
        return to_head(att_send.at[l, f], att_in.at[l, f], a_send.at[l, f], a_recv.at[l, f])

    def gate_copy(l, f):
        return to_head(gate_send.at[l, f], gate_in.at[l, f], g_send.at[l, f], g_recv.at[l, f])

    def unit(s):
        return pl.ds(pl.multiple_of(s * half, half), half)

    def unit_pair(z):
        return pl.ds(pl.multiple_of(z * pair, pair), pair)

    def near(dz, dy):
        return lax.rem(line + dz, outer) * 2 + lax.rem(side + dy, 2)

    def q_copy(l, f, s, owner):
        return pltpu.make_async_remote_copy(
            src_ref=qall.at[l, f, unit(owner)],
            dst_ref=qall.at[l, f, unit(owner)],
            send_sem=q_send.at[l, f, s],
            recv_sem=q_recv.at[l, f, owner],
            device_id={"hist": s},
            device_id_type=MESH,
        )

    def relay_copy(l, f, z):
        return pltpu.make_async_remote_copy(
            src_ref=qall.at[l, f, unit_pair(z)],
            dst_ref=qall.at[l, f, unit_pair(z)],
            send_sem=q_send.at[l, f, me],
            recv_sem=q_recv.at[l, f, 2 * z],
            device_id={"hist": near(outer - 1, 0)},
            device_id_type=MESH,
        )

    def p_copy(l, f, s, owner):
        return pltpu.make_async_remote_copy(
            src_ref=part.at[l, f, unit(s)],
            dst_ref=parts_in.at[l, f, owner],
            send_sem=p_send.at[l, f, s],
            recv_sem=p_recv.at[l, f, owner],
            device_id={"hist": s},
            device_id_type=MESH,
        )

    def targets(l, f):
        relays = RELAY[min(l, 1)][f]
        return [(dz, dy) for dz, dy in SENDS if dz != 2 or not relays]

    def send_q(l, f):
        for dz, dy in targets(l, f):
            q_copy(l, f, near(dz, dy), me).start()

    def unpack_w(l, first, last):
        halves = wl // LANES
        step = halves * 4
        if first == 0:
            load_w[l].wait()
            wide[...] = raw[l].astype(jnp.float32)
        for i in range(first, last):
            for c in range(halves):
                start = i * wl + c * LANES
                w_in[l, :, start : start + LANES] = wide[
                    pl.ds(c * 4 + i, d, stride=step), :
                ].astype(jnp.bfloat16)

    def build_tables():
        lane8 = lax.broadcasted_iota(jnp.int32, (blocks, LANES), 1)
        row8 = lax.broadcasted_iota(jnp.int32, (blocks, LANES), 0)
        lane_nb = lax.broadcasted_iota(jnp.int32, (nb, LANES), 1)
        base_of = (DH, 0)
        seen = []
        gone = []
        for base in base_of:
            held = jnp.zeros((blocks, LANES), jnp.float32)
            for m in range(micro):
                column = jnp.zeros((blocks, LANES), jnp.float32)
                for b in range(blocks):
                    value = (vis[m, b] - 1).astype(jnp.float32) * BIG
                    column = jnp.where(row8 == b, value, column)
                held = jnp.where(lane8 == base + 2 + m, column, held)
            seen.append(held)
            is_micro = (lane8 >= base + 2) & (lane8 < base + 2 + micro)
            gone.append(jnp.where(is_micro & (row8 == 0), -BIG, 0.0))
        load_r.wait()
        for l in range(layers):
            flat = jnp.concatenate([rab[l], jnp.zeros((heads, LANES - nb), jnp.float32)], axis=1)
            flat = jnp.concatenate([flat, jnp.zeros((8 - heads, LANES), jnp.float32)], axis=0)
            upright = flat.T
            for h in range(heads):
                base = base_of[h % PER]
                score = upright[:nb, h : h + 1] * 0.5
                high = score.astype(jnp.bfloat16).astype(jnp.float32)
                low = score - high
                bias = jnp.where(lane_nb == base, high, jnp.where(lane_nb == base + 1, low, 0.0))
                fill = jnp.zeros((LANES - nb - 2 * blocks, LANES), jnp.float32)
                whole = jnp.concatenate([bias, seen[h % PER], gone[h % PER], fill], axis=0)
                start = (l * heads + h) * LANES
                table[:, start : start + LANES] = whole.astype(jnp.bfloat16)

        row = lax.broadcasted_iota(jnp.int32, (LANES, hist_dev), 0)
        place = lax.broadcasted_iota(jnp.int32, (LANES, hist_dev), 1)
        load_b.wait()
        here = (
            (row == bucket[...])
            | (row == nb + place // BLOCK)
            | ((row == nb + blocks) & (place >= hlen[0]))
        )
        events[...] = jnp.where(here, 1.0, 0.0).T.astype(jnp.bfloat16)

    def augment_keys(l):
        lane_k = lax.broadcasted_iota(jnp.int32, (hist_dev, LANES), 1)
        for h in range(heads):
            start = (l * heads + h) * LANES
            extra = dot(events[...], table[:, start : start + LANES])
            p = h // PER
            tile = keys[l, :, p * LANES : (p + 1) * LANES].astype(jnp.float32)
            mine = (lane_k < DH) if h % PER == 0 else (lane_k >= DH)
            kaug[l, h] = jnp.where(mine, tile, extra).astype(jnp.bfloat16)

    lane_q = lax.broadcasted_iota(jnp.int32, (pair, LANES), 1)
    row_q = lax.broadcasted_iota(jnp.int32, (pair, LANES), 0)

    def attend(l, f, z):
        span = unit_pair(z)
        place = (z * 2 + row_q // half) * rows + f * half + row_q % half
        which = place // micro_rows
        for h in range(heads):
            p = h // PER
            base = DH if h % PER == 0 else 0
            tile = qall[l, f, span, p * LANES : (p + 1) * LANES].astype(jnp.float32)
            ones = (lane_q == base) | (lane_q == base + 1) | (lane_q == base + 2 + which)
            mine = (lane_q < DH) if h % PER == 0 else (lane_q >= DH)
            qaug[h] = jnp.where(mine, tile, jnp.where(ones, 1.0, 0.0)).astype(jnp.bfloat16)
        for p in range(pairs):
            value = vals[l, :, p * LANES : (p + 1) * LANES]
            found = []
            for e in range(PER):
                h = p * PER + e
                y = lax.dot_general(
                    qaug[h],
                    kaug[l, h],
                    (((1,), (1,)), ((), ())),
                    preferred_element_type=jnp.float32,
                ).astype(jnp.bfloat16)
                weight = y * (jnp.tanh(y) + 1.0)
                found.append(dot(weight, value))
            both = jnp.where(lane_q < DH, found[0], found[1])
            part[l, f, span, p * LANES : (p + 1) * LANES] = both.astype(jnp.bfloat16)

    block_row = lax.broadcasted_iota(jnp.int32, (wl, wl), 0) // DH
    block_col = lax.broadcasted_iota(jnp.int32, (wl, wl), 1) // DH
    same_head = jnp.where(block_row == block_col, 1.0, 0.0).astype(jnp.bfloat16)

    def normalize(l, first, last):
        mine = slice(first * half, last * half)
        x = stream[mine]
        centred = x - jnp.mean(x, axis=-1, keepdims=True)
        variance = jnp.mean(centred * centred, axis=-1, keepdims=True)
        normed[mine] = (centred * lax.rsqrt(variance + epsilon)).astype(jnp.bfloat16)

    def make_queries(l, first, last):
        mine = slice(first * half, last * half)
        queries = silu(dot(normed[mine], w_in[l, :, :wl])).astype(jnp.bfloat16)
        scaled = (queries.astype(jnp.float32) * (0.5 * DH**-0.5)).astype(jnp.bfloat16)
        for f in range(first, last):
            qall[l, f, unit(me)] = scaled[(f - first) * half : (f - first + 1) * half]
        q_own[mine] = queries

    def make_rest(l, first, last):
        mine = slice(first * half, last * half)

        def project(i):
            sums = dot(normed[mine], w_in[l, :, i * wl : (i + 1) * wl])
            return silu(sums).astype(jnp.bfloat16)

        gates = project(3)
        for f in range(first, last):
            gate_send[l, f] = gates[(f - first) * half : (f - first + 1) * half]
            gate_copy(l, f).start()
        keys_new = project(1).astype(jnp.float32)
        values_new = project(2).astype(jnp.float32)
        product = q_own[mine].astype(jnp.float32) * keys_new
        high = product.astype(jnp.bfloat16)
        low = (product - high.astype(jnp.float32)).astype(jnp.bfloat16)
        own_score = dot(high, same_head) + dot(low, same_head)
        own[mine] = silu(own_score * (DH**-0.5)) * values_new

    def add_parts(l, f):
        history = part[l, f, unit(me), :].astype(jnp.float32)
        for dz, dy in GATHER:
            s = near(dz, dy)
            p_copy(l, f, s, s).wait_recv()
            history = history + parts_in[l, f, s].astype(jnp.float32)
        att_send[l, f] = history + own[f * half : (f + 1) * half]
        att_copy(l, f).start()

    def finish(l, f):
        mine = slice(f * half, (f + 1) * half)
        if l == 0 and f == 0:
            w_copy.wait_recv()
        gate_copy(l, f).wait_recv()
        att_copy(l, f).wait_recv()
        attended, theirs = att_send[l, f], att_in[l, f]
        width = 2 * wl
        mean = (
            jnp.sum(attended, axis=-1, keepdims=True) + jnp.sum(theirs, axis=-1, keepdims=True)
        ) / width
        square = (
            jnp.sum(attended * attended, axis=-1, keepdims=True)
            + jnp.sum(theirs * theirs, axis=-1, keepdims=True)
        ) / width
        rstd = lax.rsqrt(square - mean * mean + epsilon)
        gates, gates_other = gate_send[l, f], gate_in[l, f]
        gated = ((attended - mean) * rstd * gates.astype(jnp.float32)).astype(jnp.bfloat16)
        gated_other = ((theirs - mean) * rstd * gates_other.astype(jnp.float32)).astype(
            jnp.bfloat16
        )
        x = stream[mine] + (dot(gated, w_out[l]) + dot(gated_other, w_other[l]))
        if l + 1 < layers:
            stream[mine] = x
        else:
            out[mine] = x.astype(out.dtype)

    load_c.wait()
    stream[...] = cand[...].astype(jnp.float32)
    normalize(0, 0, HALVES)
    unpack_w(0, 0, 1)
    make_queries(0, 0, HALVES)
    pl.semaphore_wait(barrier, n)
    for f in range(HALVES):
        send_q(0, f)
    unpack_w(0, 1, 4)
    make_rest(0, 0, HALVES)
    load_o.wait()
    w_copy.start()
    build_tables()
    load_k.wait()
    augment_keys(0)
    for l in range(1, layers):
        unpack_w(l, 0, 4)
    load_v.wait()

    def call(t, carry):
        l, f = t // calls, (t // outer) % HALVES
        for late in range(layers):
            first = late * calls

            @pl.when(t == first + calls - 1)
            def _(late=late):
                add_parts(late, 0)

            if late + 1 < layers:

                @pl.when(t == first + calls)
                def _(late=late):
                    finish(late, 0)
                    normalize(late + 1, 0, 1)
                    make_queries(late + 1, 0, 1)
                    send_q(late + 1, 0)
                    make_rest(late + 1, 0, 1)
                    augment_keys(late + 1)

                @pl.when(t == first + calls + SUM_B)
                def _(late=late):
                    add_parts(late, 1)

                @pl.when(t == first + calls + SUM_B + 1)
                def _(late=late):
                    finish(late, 1)
                    normalize(late + 1, 1, 2)
                    make_queries(late + 1, 1, 2)
                    send_q(late + 1, 1)
                    make_rest(late + 1, 1, 2)

        kind = jnp.minimum(l, 1)
        code = ORDERS[0] + kind * (ORDERS[1] - ORDERS[0])
        dz = lax.shift_right_logical(code, 2 * (t % calls)) & 3
        z = lax.rem(line + dz, outer)
        relayed = (lax.shift_right_logical(jnp.int32(RELAYS), 2 * kind + f) & 1) == 1

        @pl.when(dz == 0)
        def _():
            q_copy(l, f, beside, beside).wait_recv()

        @pl.when((dz == 2) & relayed)
        def _():
            relay_copy(l, f, z).wait_recv()

        @pl.when((dz != 0) & ((dz != 2) | jnp.logical_not(relayed)))
        def _():
            for i in range(2):
                q_copy(l, f, 2 * z + i, 2 * z + i).wait_recv()

        @pl.when((dz == 1) & relayed)
        def _():
            relay_copy(l, f, z).start()

        attend(l, f, z)
        for i in range(2):
            s = 2 * z + i

            @pl.when(s != me)
            def _(s=s):
                p_copy(l, f, s, me).start()

        return carry

    lax.fori_loop(0, layers * calls, call, 0)
    finish(layers - 1, 0)
    add_parts(layers - 1, 1)
    finish(layers - 1, 1)

    w_copy.wait_send()
    for l in range(layers):
        for f in range(HALVES):
            att_copy(l, f).wait_send()
            gate_copy(l, f).wait_send()
            for dz, dy in targets(l, f):
                q_copy(l, f, near(dz, dy), me).wait_send()
            if RELAY[min(l, 1)][f]:
                relay_copy(l, f, lax.rem(line + 1, outer)).wait_send()
            for j in range(1, n):
                p_copy(l, f, lax.rem(me + j, n), me).wait_send()


def pair_shards(
    n, candidates, key_cache, value_cache, w_in, w_out, rab_table, hist_len, hist_bucket, visible
):
    layers, hist_dev, wl = key_cache.shape
    rows, d = candidates.shape
    heads = wl // DH
    half = rows // HALVES
    bf16, f32 = jnp.bfloat16, jnp.float32
    vmem = pl.BlockSpec(memory_space=pltpu.VMEM)
    smem = pl.BlockSpec(memory_space=pltpu.SMEM)
    hbm = pl.BlockSpec(memory_space=pltpu.HBM)
    dma = pltpu.SemaphoreType.DMA
    wide = d * 4 * wl // LANES
    return pl.pallas_call(
        functools.partial(pair_kernel, n),
        out_shape=jax.ShapeDtypeStruct((rows, d), bf16),
        in_specs=[hbm, hbm, hbm, hbm, hbm, hbm, hbm, smem, smem],
        out_specs=vmem,
        scratch_shapes=[
            pltpu.VMEM((rows, d), bf16),
            pltpu.VMEM((layers, wide, LANES), bf16),
            pltpu.VMEM((wide, LANES), f32),
            pltpu.VMEM((layers, d, 4 * wl), bf16),
            pltpu.VMEM(w_out.shape, bf16),
            pltpu.VMEM((layers, heads, rab_table.shape[1]), f32),
            pltpu.VMEM((1, hist_dev), jnp.int32),
            pltpu.VMEM((layers, hist_dev, wl), bf16),
            pltpu.VMEM((layers, hist_dev, wl), bf16),
            pltpu.VMEM((layers, heads, hist_dev, LANES), bf16),
            pltpu.VMEM((LANES, layers * heads * LANES), bf16),
            pltpu.VMEM((hist_dev, LANES), bf16),
            pltpu.VMEM(w_out.shape, bf16),
            pltpu.VMEM((layers, HALVES, n * half, wl), bf16),
            pltpu.VMEM((heads, 2 * half, LANES), bf16),
            pltpu.VMEM((layers, HALVES, n * half, wl), bf16),
            pltpu.VMEM((layers, HALVES, n, half, wl), bf16),
            pltpu.VMEM((rows, d), f32),
            pltpu.VMEM((rows, d), bf16),
            pltpu.VMEM((rows, wl), bf16),
            pltpu.VMEM((rows, wl), f32),
            pltpu.VMEM((layers, HALVES, half, wl), f32),
            pltpu.VMEM((layers, HALVES, half, wl), f32),
            pltpu.VMEM((layers, HALVES, half, wl), bf16),
            pltpu.VMEM((layers, HALVES, half, wl), bf16),
            dma((6 + layers,)),
            dma((layers, HALVES, n)),
            dma((layers, HALVES, n)),
            dma((layers, HALVES, n)),
            dma((layers, HALVES, n)),
            dma((layers, HALVES)),
            dma((layers, HALVES)),
            dma((layers, HALVES)),
            dma((layers, HALVES)),
            dma,
            dma,
        ],
        compiler_params=pltpu.CompilerParams(
            collective_id=1, has_side_effects=True, vmem_limit_bytes=60 * 1024 * 1024
        ),
    )(
        candidates,
        w_in.reshape(layers, d, 4, wl // LANES, LANES)
        .transpose(0, 1, 3, 2, 4)
        .reshape(layers, wide, LANES),
        key_cache,
        value_cache,
        w_out,
        rab_table.transpose(0, 2, 1),
        hist_bucket.reshape(1, hist_dev),
        hist_len,
        visible,
    )


def in_pairs(mesh):
    n = mesh.shape["hist"]
    if n != 8:
        return False
    index = [slice(None) if name == "hist" else 0 for name in mesh.axis_names]
    spots = [getattr(device, "coords", None) for device in mesh.devices[tuple(index)][:3]]
    if any(spot is None for spot in spots):
        return False
    apart = [sum(abs(a - b) for a, b in zip(spots[0], spot)) for spot in spots[1:]]
    return apart == [1, 1]


def solution(mesh):
    placed = (
        P(("users", "hist"), None),
        P(None, ("users", "hist"), "head"),
        P(None, ("users", "hist"), "head"),
        P(None, None, None, "head"),
        P(None, "head", None),
        P(None, None, "head"),
        P(("users", "hist")),
        P(("users", "hist")),
        P(None, ("users", "hist")),
    )
    chosen = pair_shards if in_pairs(mesh) else shards
    return jax.shard_map(
        functools.partial(chosen, mesh.shape["hist"]),
        mesh=mesh,
        in_specs=placed,
        out_specs=P(("users", "hist"), None),
        check_vma=False,
    )
```

```python
import functools

import jax
import jax.numpy as jnp
from jax import lax
from jax.experimental import pallas as pl
from jax.experimental.pallas import tpu as pltpu
from jax.sharding import PartitionSpec as P

DH = 64
BLOCK = 256
LANES = 128
PER = LANES // DH
GROUP_ROWS = 256
KEY_CHUNK = 2048
BIG = 16384.0
MESH = pl.DeviceIdType.MESH
HALVES = 2
SENDS = ((3, 0), (3, 1), (0, 1), (1, 0), (1, 1))
GATHER = ((3, 0), (3, 1), (1, 0), (1, 1), (2, 0), (2, 1), (0, 1))
ORDER = ((1, 3, 0, 2, 2, 1, 3, 0), (1, 3, 0, 2, 1, 3, 0, 2))
ORDERS = [sum(dz << (2 * t) for t, dz in enumerate(order)) for order in ORDER]
FORWARD = (1, 3)
SUM_A = (7, 7)
SUM_B = 0
END_B = 0

epsilon = 1e-05


def silu(v):
    return v / (1.0 + jnp.exp(-v))


def dot(a, b):
    return jnp.dot(a, b, preferred_element_type=jnp.float32)


def kernel(
    n,
    cand_hbm,
    w_hbm,
    key_hbm,
    val_hbm,
    wo_hbm,
    rab_hbm,
    bucket_hbm,
    hlen,
    vis,
    out,
    cand,
    raw,
    wide,
    w_in,
    w_out,
    rab,
    bucket,
    keys,
    vals,
    kaug,
    table,
    events,
    w_other,
    qall,
    qaug,
    part,
    parts_in,
    acc,
    att_send,
    att_in,
    gate_send,
    gate_in,
    load_sem,
    q_send,
    q_recv,
    p_send,
    p_recv,
    h_send,
    h_recv,
):
    me = lax.axis_index("hist")
    other = 1 - lax.axis_index("head")
    layers, hist_dev, wl = key_hbm.shape
    rows, d = cand.shape
    heads = wl // DH
    parts_w = 4
    pairs = wl // LANES
    nb = rab.shape[2]
    micro, blocks = vis.shape
    total = n * rows
    micro_rows = total // micro
    group_rows = min(GROUP_ROWS, total)
    per_group = group_rows // rows
    groups = n // per_group
    key_chunk = min(KEY_CHUNK, hist_dev)

    load_k = pltpu.make_async_copy(key_hbm, keys, load_sem.at[0])
    load_v = pltpu.make_async_copy(val_hbm, vals, load_sem.at[1])
    load_c = pltpu.make_async_copy(cand_hbm, cand, load_sem.at[2])
    load_w = [
        pltpu.make_async_copy(w_hbm.at[l], raw.at[l], load_sem.at[3 + l]) for l in range(layers)
    ]
    load_o = pltpu.make_async_copy(wo_hbm, w_out, load_sem.at[3 + layers])
    load_r = pltpu.make_async_copy(rab_hbm, rab, load_sem.at[4 + layers])
    load_b = pltpu.make_async_copy(bucket_hbm, bucket, load_sem.at[5 + layers])
    load_c.start()
    load_w[0].start()
    load_b.start()
    load_r.start()
    load_k.start()
    load_o.start()
    load_v.start()
    for copy in load_w[1:]:
        copy.start()

    barrier = pltpu.get_barrier_semaphore()
    for j in range(1, n):
        pl.semaphore_signal(
            barrier, inc=1, device_id={"hist": lax.rem(me + j, n)}, device_id_type=MESH
        )
    pl.semaphore_signal(barrier, inc=1, device_id={"head": other}, device_id_type=MESH)

    def to_head(src, dst, index):
        return pltpu.make_async_remote_copy(
            src_ref=src,
            dst_ref=dst,
            send_sem=h_send.at[index],
            recv_sem=h_recv.at[index],
            device_id={"head": other},
            device_id_type=MESH,
        )

    def unpack_w(l):
        halves = wl // LANES
        step = halves * parts_w
        wide[...] = raw[l].astype(jnp.float32)
        for i in range(parts_w):
            for c in range(halves):
                start = i * wl + c * LANES
                w_in[:, start : start + LANES] = wide[
                    pl.ds(c * parts_w + i, d, stride=step), :
                ].astype(jnp.bfloat16)

    def row_of(s):
        return pl.ds(pl.multiple_of(s * rows, rows), rows)

    def q_copy(l, s, owner):
        return pltpu.make_async_remote_copy(
            src_ref=qall.at[l, row_of(owner)],
            dst_ref=qall.at[l, row_of(owner)],
            send_sem=q_send.at[l, s],
            recv_sem=q_recv.at[l, owner],
            device_id={"hist": s},
            device_id_type=MESH,
        )

    def p_copy(l, s, owner):
        return pltpu.make_async_remote_copy(
            src_ref=part.at[l, row_of(s)],
            dst_ref=parts_in.at[l, owner],
            send_sem=p_send.at[l, s],
            recv_sem=p_recv.at[l, owner],
            device_id={"hist": s},
            device_id_type=MESH,
        )

    def build_keys():
        lane = lax.broadcasted_iota(jnp.int32, (LANES, LANES), 1)
        lane8 = lax.broadcasted_iota(jnp.int32, (blocks, LANES), 1)
        row8 = lax.broadcasted_iota(jnp.int32, (blocks, LANES), 0)
        base_of = (DH, 0)
        seen = []
        gone = []
        for base in base_of:
            held = jnp.zeros((blocks, LANES), jnp.float32)
            for m in range(micro):
                column = jnp.zeros((blocks, LANES), jnp.float32)
                for b in range(blocks):
                    value = (vis[m, b] - 1).astype(jnp.float32) * BIG
                    column = jnp.where(row8 == b, value, column)
                held = jnp.where(lane8 == base + 2 + m, column, held)
            seen.append(held)
            is_micro = (lane8 >= base + 2) & (lane8 < base + 2 + micro)
            gone.append(jnp.where(is_micro & (row8 == 0), -BIG, 0.0))
        for l in range(layers):
            flat = jnp.concatenate([rab[l], jnp.zeros((heads, LANES - nb), jnp.float32)], axis=1)
            flat = jnp.concatenate([flat, jnp.zeros((8 - heads, LANES), jnp.float32)], axis=0)
            upright = flat.T
            for h in range(heads):
                base = base_of[h % PER]
                half = upright[:nb, h : h + 1] * 0.5
                high = half.astype(jnp.bfloat16).astype(jnp.float32)
                low = half - high
                lane_nb = lane[:nb]
                bias = jnp.where(lane_nb == base, high, jnp.where(lane_nb == base + 1, low, 0.0))
                fill = jnp.zeros((LANES - nb - 2 * blocks, LANES), jnp.float32)
                whole = jnp.concatenate([bias, seen[h % PER], gone[h % PER], fill], axis=0)
                start = (l * heads + h) * LANES
                table[:, start : start + LANES] = whole.astype(jnp.bfloat16)

        row = lax.broadcasted_iota(jnp.int32, (LANES, key_chunk), 0)
        spot = lax.broadcasted_iota(jnp.int32, (LANES, key_chunk), 1)
        lane_k = lax.broadcasted_iota(jnp.int32, (key_chunk, LANES), 1)
        length = hlen[0]
        for c in range(hist_dev // key_chunk):
            span = slice(c * key_chunk, (c + 1) * key_chunk)
            place = spot + c * key_chunk
            here = (
                (row == bucket[:, span])
                | (row == nb + place // BLOCK)
                | ((row == nb + blocks) & (place >= length))
            )
            events[span, :] = jnp.where(here, 1.0, 0.0).T.astype(jnp.bfloat16)
        load_k.wait()

        def chunk(c, carry):
            span = pl.ds(pl.multiple_of(c * key_chunk, key_chunk), key_chunk)
            spread = events[span, :]
            for l in range(layers):
                for h in range(heads):
                    start = (l * heads + h) * LANES
                    extra = dot(spread, table[:, start : start + LANES])
                    p = h // PER
                    tile = keys[l, span, p * LANES : (p + 1) * LANES].astype(jnp.float32)
                    mine = (lane_k < DH) if h % PER == 0 else (lane_k >= DH)
                    kaug[l, h, span, :] = jnp.where(mine, tile, extra).astype(jnp.bfloat16)
            return carry

        lax.fori_loop(0, hist_dev // key_chunk, chunk, 0)

    lane_q = lax.broadcasted_iota(jnp.int32, (group_rows, LANES), 1)
    row_q = lax.broadcasted_iota(jnp.int32, (group_rows, LANES), 0)
    lane_a = lax.broadcasted_iota(jnp.int32, (group_rows, LANES), 1)

    def attend(l, g):
        span = pl.ds(pl.multiple_of(g * group_rows, group_rows), group_rows)
        which = (row_q + g * group_rows) // micro_rows
        for h in range(heads):
            p = h // PER
            base = DH if h % PER == 0 else 0
            tile = qall[l, span, p * LANES : (p + 1) * LANES].astype(jnp.float32)
            ones = (lane_q == base) | (lane_q == base + 1) | (lane_q == base + 2 + which)
            mine = (lane_q < DH) if h % PER == 0 else (lane_q >= DH)
            qaug[h] = jnp.where(mine, tile, jnp.where(ones, 1.0, 0.0)).astype(jnp.bfloat16)
        acc[...] = jnp.zeros_like(acc)

        def chunk(c, carry):
            keys_at = pl.ds(pl.multiple_of(c * key_chunk, key_chunk), key_chunk)
            for p in range(pairs):
                value = vals[l, keys_at, p * LANES : (p + 1) * LANES]
                found = []
                for e in range(PER):
                    h = p * PER + e
                    y = lax.dot_general(
                        qaug[h],
                        kaug[l, h, keys_at, :],
                        (((1,), (1,)), ((), ())),
                        preferred_element_type=jnp.float32,
                    ).astype(jnp.bfloat16)
                    weight = y * (jnp.tanh(y) + 1.0)
                    found.append(dot(weight, value))
                acc[:, p * LANES : (p + 1) * LANES] += jnp.where(lane_a < DH, found[0], found[1])
            return carry

        lax.fori_loop(0, hist_dev // key_chunk, chunk, 0)
        part[l, span, :] = acc[...].astype(jnp.bfloat16)

    block_row = lax.broadcasted_iota(jnp.int32, (wl, wl), 0) // DH
    block_col = lax.broadcasted_iota(jnp.int32, (wl, wl), 1) // DH
    same_head = jnp.where(block_row == block_col, 1.0, 0.0).astype(jnp.bfloat16)

    load_c.wait()
    stream = cand[...].astype(jnp.float32)
    for l in range(layers):
        load_w[l].wait()
        unpack_w(l)
        average = jnp.mean(stream, axis=-1, keepdims=True)
        centred = stream - average
        variance = jnp.mean(centred * centred, axis=-1, keepdims=True)
        normed = (centred * lax.rsqrt(variance + epsilon)).astype(jnp.bfloat16)

        def project(i):
            return silu(dot(normed, w_in[:, i * wl : (i + 1) * wl])).astype(jnp.bfloat16)

        queries = project(0).astype(jnp.float32)
        qall[l, row_of(me), :] = (queries * (0.5 * DH**-0.5)).astype(jnp.bfloat16)
        if l == 0:
            pl.semaphore_wait(barrier, n)
        for j in range(1, n):
            q_copy(l, lax.rem(me + j, n), me).start()
        keys_new = project(1).astype(jnp.float32)
        values_new = project(2).astype(jnp.float32)
        gates = project(3)
        gate_send[l] = gates
        gate_copy = to_head(gate_send.at[l], gate_in.at[l], 2 * l)
        gate_copy.start()
        if l == 0:
            load_o.wait()
            w_copy = to_head(w_out, w_other, 2 * layers)
            w_copy.start()
        product = queries * keys_new
        high = product.astype(jnp.bfloat16)
        low = (product - high.astype(jnp.float32)).astype(jnp.bfloat16)
        own_score = dot(high, same_head) + dot(low, same_head)
        own = silu(own_score * (DH**-0.5)) * values_new
        if l == 0:
            load_r.wait()
            load_b.wait()
            build_keys()
            load_v.wait()

        def group(t, carry):
            g = lax.rem(me // per_group + t, groups)
            for i in range(per_group):
                s = g * per_group + i

                @pl.when(s != me)
                def _():
                    q_copy(l, s, s).wait_recv()

            attend(l, g)
            for i in range(per_group):
                s = g * per_group + i

                @pl.when(s != me)
                def _():
                    p_copy(l, s, me).start()

            return carry

        lax.fori_loop(0, groups, group, 0)
        history = part[l, row_of(me), :].astype(jnp.float32)
        for j in range(1, n):
            s = lax.rem(me + j, n)
            p_copy(l, s, s).wait_recv()
            history = history + parts_in[l, s].astype(jnp.float32)
        attended = history + own
        att_send[l] = attended
        att_copy = to_head(att_send.at[l], att_in.at[l], 2 * l + 1)
        att_copy.start()
        if l == 0:
            w_copy.wait_recv()
        gate_copy.wait_recv()
        att_copy.wait_recv()
        theirs = att_in[l]
        width = 2 * wl
        mean = (
            jnp.sum(attended, axis=-1, keepdims=True) + jnp.sum(theirs, axis=-1, keepdims=True)
        ) / width
        square = (
            jnp.sum(attended * attended, axis=-1, keepdims=True)
            + jnp.sum(theirs * theirs, axis=-1, keepdims=True)
        ) / width
        rstd = lax.rsqrt(square - mean * mean + epsilon)
        gated = ((attended - mean) * rstd * gates.astype(jnp.float32)).astype(jnp.bfloat16)
        gated_other = ((theirs - mean) * rstd * gate_in[l].astype(jnp.float32)).astype(
            jnp.bfloat16
        )
        stream = stream + (dot(gated, w_out[l]) + dot(gated_other, w_other[l]))
        gate_copy.wait_send()
        att_copy.wait_send()
        if l == 0:
            w_copy.wait_send()
        for j in range(1, n):
            s = lax.rem(me + j, n)
            q_copy(l, s, me).wait_send()
            p_copy(l, s, me).wait_send()
    out[...] = stream.astype(out.dtype)


def shards(
    n, candidates, key_cache, value_cache, w_in, w_out, rab_table, hist_len, hist_bucket, visible
):
    layers, hist_dev, wl = key_cache.shape
    rows, d = candidates.shape
    heads = wl // DH
    total = n * rows
    group_rows = min(GROUP_ROWS, total)
    bf16, f32 = jnp.bfloat16, jnp.float32
    vmem = pl.BlockSpec(memory_space=pltpu.VMEM)
    smem = pl.BlockSpec(memory_space=pltpu.SMEM)
    hbm = pl.BlockSpec(memory_space=pltpu.HBM)
    dma = pltpu.SemaphoreType.DMA
    return pl.pallas_call(
        functools.partial(kernel, n),
        out_shape=jax.ShapeDtypeStruct((rows, d), bf16),
        in_specs=[hbm, hbm, hbm, hbm, hbm, hbm, hbm, smem, smem],
        out_specs=vmem,
        scratch_shapes=[
            pltpu.VMEM((rows, d), bf16),
            pltpu.VMEM((layers, d * 4 * wl // LANES, LANES), bf16),
            pltpu.VMEM((d * 4 * wl // LANES, LANES), f32),
            pltpu.VMEM((d, 4 * wl), bf16),
            pltpu.VMEM(w_out.shape, bf16),
            pltpu.VMEM((layers, heads, rab_table.shape[1]), f32),
            pltpu.VMEM((1, hist_dev), jnp.int32),
            pltpu.VMEM((layers, hist_dev, wl), bf16),
            pltpu.VMEM((layers, hist_dev, wl), bf16),
            pltpu.VMEM((layers, heads, hist_dev, LANES), bf16),
            pltpu.VMEM((LANES, layers * heads * LANES), bf16),
            pltpu.VMEM((hist_dev, LANES), bf16),
            pltpu.VMEM(w_out.shape, bf16),
            pltpu.VMEM((layers, total, wl), bf16),
            pltpu.VMEM((heads, group_rows, LANES), bf16),
            pltpu.VMEM((layers, total, wl), bf16),
            pltpu.VMEM((layers, n, rows, wl), bf16),
            pltpu.VMEM((group_rows, wl), f32),
            pltpu.VMEM((layers, rows, wl), f32),
            pltpu.VMEM((layers, rows, wl), f32),
            pltpu.VMEM((layers, rows, wl), bf16),
            pltpu.VMEM((layers, rows, wl), bf16),
            dma((6 + layers,)),
            dma((layers, n)),
            dma((layers, n)),
            dma((layers, n)),
            dma((layers, n)),
            dma((2 * layers + 1,)),
            dma((2 * layers + 1,)),
        ],
        compiler_params=pltpu.CompilerParams(
            collective_id=0, has_side_effects=True, vmem_limit_bytes=60 * 1024 * 1024
        ),
    )(
        candidates,
        w_in.reshape(layers, d, 4, wl // LANES, LANES)
        .transpose(0, 1, 3, 2, 4)
        .reshape(layers, d * 4 * wl // LANES, LANES),
        key_cache,
        value_cache,
        w_out,
        rab_table.transpose(0, 2, 1),
        hist_bucket.reshape(1, hist_dev),
        hist_len,
        visible,
    )


def pair_kernel(
    n,
    cand_hbm,
    w_hbm,
    key_hbm,
    val_hbm,
    wo_hbm,
    rab_hbm,
    bucket_hbm,
    hlen,
    vis,
    out,
    cand,
    raw,
    wide,
    w_in,
    w_out,
    rab,
    bucket,
    keys,
    vals,
    kaug,
    table,
    events,
    w_other,
    qall,
    qaug,
    part,
    parts_in,
    stream,
    normed,
    q_own,
    own,
    att_send,
    att_in,
    gate_send,
    gate_in,
    load_sem,
    q_send,
    q_recv,
    p_send,
    p_recv,
    a_send,
    a_recv,
    g_send,
    g_recv,
    w_send,
    w_recv,
):
    me = lax.axis_index("hist")
    other = 1 - lax.axis_index("head")
    layers, hist_dev, wl = key_hbm.shape
    rows, d = cand.shape
    heads = wl // DH
    pairs = wl // LANES
    nb = rab.shape[2]
    micro, blocks = vis.shape
    micro_rows = n * rows // micro
    half = rows // HALVES
    pair = 2 * half
    outer = n // 2
    calls = HALVES * outer
    line, side = me // 2, lax.rem(me, 2)
    beside = line * 2 + 1 - side

    load_c = pltpu.make_async_copy(cand_hbm, cand, load_sem.at[0])
    load_w = [
        pltpu.make_async_copy(w_hbm.at[l], raw.at[l], load_sem.at[6 + l]) for l in range(layers)
    ]
    load_k = pltpu.make_async_copy(key_hbm, keys, load_sem.at[1])
    load_v = pltpu.make_async_copy(val_hbm, vals, load_sem.at[2])
    load_o = pltpu.make_async_copy(wo_hbm, w_out, load_sem.at[3])
    load_r = pltpu.make_async_copy(rab_hbm, rab, load_sem.at[4])
    load_b = pltpu.make_async_copy(bucket_hbm, bucket, load_sem.at[5])
    load_c.start()
    load_w[0].start()

    barrier = pltpu.get_barrier_semaphore()
    for j in range(1, n):
        pl.semaphore_signal(
            barrier, inc=1, device_id={"hist": lax.rem(me + j, n)}, device_id_type=MESH
        )
    pl.semaphore_signal(barrier, inc=1, device_id={"head": other}, device_id_type=MESH)

    load_b.start()
    load_r.start()
    load_k.start()
    load_o.start()
    load_v.start()
    for copy in load_w[1:]:
        copy.start()

    def to_head(src, dst, send, recv):
        return pltpu.make_async_remote_copy(
            src_ref=src,
            dst_ref=dst,
            send_sem=send,
            recv_sem=recv,
            device_id={"head": other},
            device_id_type=MESH,
        )

    w_copy = to_head(w_out, w_other, w_send, w_recv)

    def att_copy(l, f):
        return to_head(att_send.at[l, f], att_in.at[l, f], a_send.at[l, f], a_recv.at[l, f])

    def gate_copy(l, f):
        return to_head(gate_send.at[l, f], gate_in.at[l, f], g_send.at[l, f], g_recv.at[l, f])

    def unit(s):
        return pl.ds(pl.multiple_of(s * half, half), half)

    def unit_pair(z):
        return pl.ds(pl.multiple_of(z * pair, pair), pair)

    def near(dz, dy):
        return lax.rem(line + dz, outer) * 2 + lax.rem(side + dy, 2)

    def q_copy(l, f, s, owner):
        return pltpu.make_async_remote_copy(
            src_ref=qall.at[l, f, unit(owner)],
            dst_ref=qall.at[l, f, unit(owner)],
            send_sem=q_send.at[l, f, s],
            recv_sem=q_recv.at[l, f, owner],
            device_id={"hist": s},
            device_id_type=MESH,
        )

    def relay_copy(l, f, z):
        return pltpu.make_async_remote_copy(
            src_ref=qall.at[l, f, unit_pair(z)],
            dst_ref=qall.at[l, f, unit_pair(z)],
            send_sem=q_send.at[l, f, me],
            recv_sem=q_recv.at[l, f, 2 * z],
            device_id={"hist": near(outer - 1, 0)},
            device_id_type=MESH,
        )

    def p_copy(l, f, s, owner):
        return pltpu.make_async_remote_copy(
            src_ref=part.at[l, f, unit(s)],
            dst_ref=parts_in.at[l, f, owner],
            send_sem=p_send.at[l, f, s],
            recv_sem=p_recv.at[l, f, owner],
            device_id={"hist": s},
            device_id_type=MESH,
        )

    def send_q(l, f):
        for dz, dy in SENDS:
            q_copy(l, f, near(dz, dy), me).start()

    def unpack_w(l, first, last):
        halves = wl // LANES
        step = halves * 4
        if first == 0:
            load_w[l].wait()
            wide[...] = raw[l].astype(jnp.float32)
        for i in range(first, last):
            for c in range(halves):
                start = i * wl + c * LANES
                w_in[l, :, start : start + LANES] = wide[
                    pl.ds(c * 4 + i, d, stride=step), :
                ].astype(jnp.bfloat16)

    def build_tables():
        lane8 = lax.broadcasted_iota(jnp.int32, (blocks, LANES), 1)
        row8 = lax.broadcasted_iota(jnp.int32, (blocks, LANES), 0)
        lane_nb = lax.broadcasted_iota(jnp.int32, (nb, LANES), 1)
        base_of = (DH, 0)
        seen = []
        gone = []
        for base in base_of:
            held = jnp.zeros((blocks, LANES), jnp.float32)
            for m in range(micro):
                column = jnp.zeros((blocks, LANES), jnp.float32)
                for b in range(blocks):
                    value = (vis[m, b] - 1).astype(jnp.float32) * BIG
                    column = jnp.where(row8 == b, value, column)
                held = jnp.where(lane8 == base + 2 + m, column, held)
            seen.append(held)
            is_micro = (lane8 >= base + 2) & (lane8 < base + 2 + micro)
            gone.append(jnp.where(is_micro & (row8 == 0), -BIG, 0.0))
        load_r.wait()
        for l in range(layers):
            flat = jnp.concatenate([rab[l], jnp.zeros((heads, LANES - nb), jnp.float32)], axis=1)
            flat = jnp.concatenate([flat, jnp.zeros((8 - heads, LANES), jnp.float32)], axis=0)
            upright = flat.T
            for h in range(heads):
                base = base_of[h % PER]
                score = upright[:nb, h : h + 1] * 0.5
                high = score.astype(jnp.bfloat16).astype(jnp.float32)
                low = score - high
                bias = jnp.where(lane_nb == base, high, jnp.where(lane_nb == base + 1, low, 0.0))
                fill = jnp.zeros((LANES - nb - 2 * blocks, LANES), jnp.float32)
                whole = jnp.concatenate([bias, seen[h % PER], gone[h % PER], fill], axis=0)
                start = (l * heads + h) * LANES
                table[:, start : start + LANES] = whole.astype(jnp.bfloat16)

        row = lax.broadcasted_iota(jnp.int32, (LANES, hist_dev), 0)
        place = lax.broadcasted_iota(jnp.int32, (LANES, hist_dev), 1)
        load_b.wait()
        here = (
            (row == bucket[...])
            | (row == nb + place // BLOCK)
            | ((row == nb + blocks) & (place >= hlen[0]))
        )
        events[...] = jnp.where(here, 1.0, 0.0).T.astype(jnp.bfloat16)

    def augment_keys(l):
        lane_k = lax.broadcasted_iota(jnp.int32, (hist_dev, LANES), 1)
        for h in range(heads):
            start = (l * heads + h) * LANES
            extra = dot(events[...], table[:, start : start + LANES])
            p = h // PER
            tile = keys[l, :, p * LANES : (p + 1) * LANES].astype(jnp.float32)
            mine = (lane_k < DH) if h % PER == 0 else (lane_k >= DH)
            kaug[l, h] = jnp.where(mine, tile, extra).astype(jnp.bfloat16)

    lane_q = lax.broadcasted_iota(jnp.int32, (pair, LANES), 1)
    row_q = lax.broadcasted_iota(jnp.int32, (pair, LANES), 0)

    def attend(l, f, z):
        span = unit_pair(z)
        place = (z * 2 + row_q // half) * rows + f * half + row_q % half
        which = place // micro_rows
        for h in range(heads):
            p = h // PER
            base = DH if h % PER == 0 else 0
            tile = qall[l, f, span, p * LANES : (p + 1) * LANES].astype(jnp.float32)
            ones = (lane_q == base) | (lane_q == base + 1) | (lane_q == base + 2 + which)
            mine = (lane_q < DH) if h % PER == 0 else (lane_q >= DH)
            qaug[h] = jnp.where(mine, tile, jnp.where(ones, 1.0, 0.0)).astype(jnp.bfloat16)
        for p in range(pairs):
            value = vals[l, :, p * LANES : (p + 1) * LANES]
            found = []
            for e in range(PER):
                h = p * PER + e
                y = lax.dot_general(
                    qaug[h],
                    kaug[l, h],
                    (((1,), (1,)), ((), ())),
                    preferred_element_type=jnp.float32,
                ).astype(jnp.bfloat16)
                weight = y * (jnp.tanh(y) + 1.0)
                found.append(dot(weight, value))
            both = jnp.where(lane_q < DH, found[0], found[1])
            part[l, f, span, p * LANES : (p + 1) * LANES] = both.astype(jnp.bfloat16)

    block_row = lax.broadcasted_iota(jnp.int32, (wl, wl), 0) // DH
    block_col = lax.broadcasted_iota(jnp.int32, (wl, wl), 1) // DH
    same_head = jnp.where(block_row == block_col, 1.0, 0.0).astype(jnp.bfloat16)

    def normalize(l, first, last):
        mine = slice(first * half, last * half)
        x = stream[mine]
        centred = x - jnp.mean(x, axis=-1, keepdims=True)
        variance = jnp.mean(centred * centred, axis=-1, keepdims=True)
        normed[mine] = (centred * lax.rsqrt(variance + epsilon)).astype(jnp.bfloat16)

    def make_queries(l, first, last):
        mine = slice(first * half, last * half)
        queries = silu(dot(normed[mine], w_in[l, :, :wl])).astype(jnp.bfloat16)
        scaled = (queries.astype(jnp.float32) * (0.5 * DH**-0.5)).astype(jnp.bfloat16)
        for f in range(first, last):
            qall[l, f, unit(me)] = scaled[(f - first) * half : (f - first + 1) * half]
        q_own[mine] = queries

    def make_rest(l, first, last):
        mine = slice(first * half, last * half)

        def project(i):
            sums = dot(normed[mine], w_in[l, :, i * wl : (i + 1) * wl])
            return silu(sums).astype(jnp.bfloat16)

        gates = project(3)
        for f in range(first, last):
            gate_send[l, f] = gates[(f - first) * half : (f - first + 1) * half]
            gate_copy(l, f).start()
        keys_new = project(1).astype(jnp.float32)
        values_new = project(2).astype(jnp.float32)
        product = q_own[mine].astype(jnp.float32) * keys_new
        high = product.astype(jnp.bfloat16)
        low = (product - high.astype(jnp.float32)).astype(jnp.bfloat16)
        own_score = dot(high, same_head) + dot(low, same_head)
        own[mine] = silu(own_score * (DH**-0.5)) * values_new

    def add_parts(l, f):
        history = part[l, f, unit(me), :].astype(jnp.float32)
        for dz, dy in GATHER:
            s = near(dz, dy)
            p_copy(l, f, s, s).wait_recv()
            history = history + parts_in[l, f, s].astype(jnp.float32)
        att_send[l, f] = history + own[f * half : (f + 1) * half]
        att_copy(l, f).start()

    def finish(l, f):
        mine = slice(f * half, (f + 1) * half)
        if l == 0 and f == 0:
            w_copy.wait_recv()
        gate_copy(l, f).wait_recv()
        att_copy(l, f).wait_recv()
        attended, theirs = att_send[l, f], att_in[l, f]
        width = 2 * wl
        mean = (
            jnp.sum(attended, axis=-1, keepdims=True) + jnp.sum(theirs, axis=-1, keepdims=True)
        ) / width
        square = (
            jnp.sum(attended * attended, axis=-1, keepdims=True)
            + jnp.sum(theirs * theirs, axis=-1, keepdims=True)
        ) / width
        rstd = lax.rsqrt(square - mean * mean + epsilon)
        gates, gates_other = gate_send[l, f], gate_in[l, f]
        gated = ((attended - mean) * rstd * gates.astype(jnp.float32)).astype(jnp.bfloat16)
        gated_other = ((theirs - mean) * rstd * gates_other.astype(jnp.float32)).astype(
            jnp.bfloat16
        )
        x = stream[mine] + (dot(gated, w_out[l]) + dot(gated_other, w_other[l]))
        if l + 1 < layers:
            stream[mine] = x
        else:
            out[mine] = x.astype(out.dtype)

    load_c.wait()
    stream[...] = cand[...].astype(jnp.float32)
    normalize(0, 0, HALVES)
    unpack_w(0, 0, 1)
    make_queries(0, 0, HALVES)

    def prepare():
        build_tables()
        load_k.wait()
        augment_keys(0)
        for l in range(1, layers):
            unpack_w(l, 0, 4)

    pl.semaphore_wait(barrier, n)
    for f in range(HALVES):
        send_q(0, f)
    unpack_w(0, 1, 4)
    make_rest(0, 0, HALVES)
    load_o.wait()
    w_copy.start()
    prepare()
    load_v.wait()

    def call(t, carry):
        l, f = t // calls, (t // outer) % HALVES
        for late in range(layers):
            first = late * calls

            if SUM_A[min(late, 1)] < calls:

                @pl.when(t == first + SUM_A[min(late, 1)])
                def _(late=late):
                    add_parts(late, 0)

            if late + 1 < layers:

                @pl.when(t == first + calls)
                def _(late=late):
                    if SUM_A[min(late, 1)] == calls:
                        add_parts(late, 0)
                    finish(late, 0)
                    normalize(late + 1, 0, 1)
                    make_queries(late + 1, 0, 1)
                    send_q(late + 1, 0)
                    make_rest(late + 1, 0, 1)
                    augment_keys(late + 1)

                @pl.when(t == first + calls + SUM_B)
                def _(late=late):
                    add_parts(late, 1)

                @pl.when(t == first + calls + END_B)
                def _(late=late):
                    finish(late, 1)
                    normalize(late + 1, 1, 2)
                    make_queries(late + 1, 1, 2)
                    send_q(late + 1, 1)
                    make_rest(late + 1, 1, 2)

        kind = jnp.minimum(l, 1)
        code = ORDERS[0] + kind * (ORDERS[1] - ORDERS[0])
        dz = lax.shift_right_logical(code, 2 * (t % calls)) & 3
        z = lax.rem(line + dz, outer)
        @pl.when(dz == 0)
        def _():
            q_copy(l, f, beside, beside).wait_recv()

        @pl.when(t % calls == FORWARD[0] + kind * (FORWARD[1] - FORWARD[0]))
        def _():
            after = lax.rem(line + 1, outer)
            for i in range(2):
                q_copy(l, 1, 2 * after + i, 2 * after + i).wait_recv()
            relay_copy(l, 1, after).start()

        @pl.when(dz == 2)
        def _():
            relay_copy(l, f, z).wait_recv()

        @pl.when((dz == 3) | ((dz == 1) & (f == 0)))
        def _():
            for i in range(2):
                q_copy(l, f, 2 * z + i, 2 * z + i).wait_recv()

        @pl.when((dz == 1) & (f == 0))
        def _():
            relay_copy(l, f, z).start()

        attend(l, f, z)
        for i in range(2):
            s = 2 * z + i

            @pl.when(s != me)
            def _(s=s):
                p_copy(l, f, s, me).start()

        return carry

    lax.fori_loop(0, layers * calls, call, 0)
    if SUM_A[min(layers - 1, 1)] == calls:
        add_parts(layers - 1, 0)
    finish(layers - 1, 0)
    add_parts(layers - 1, 1)
    finish(layers - 1, 1)

    w_copy.wait_send()
    for l in range(layers):
        for f in range(HALVES):
            att_copy(l, f).wait_send()
            gate_copy(l, f).wait_send()
            for dz, dy in SENDS:
                q_copy(l, f, near(dz, dy), me).wait_send()
            relay_copy(l, f, lax.rem(line + 1, outer)).wait_send()
            for j in range(1, n):
                p_copy(l, f, lax.rem(me + j, n), me).wait_send()


def pair_shards(
    n, candidates, key_cache, value_cache, w_in, w_out, rab_table, hist_len, hist_bucket, visible
):
    layers, hist_dev, wl = key_cache.shape
    rows, d = candidates.shape
    heads = wl // DH
    half = rows // HALVES
    bf16, f32 = jnp.bfloat16, jnp.float32
    vmem = pl.BlockSpec(memory_space=pltpu.VMEM)
    smem = pl.BlockSpec(memory_space=pltpu.SMEM)
    hbm = pl.BlockSpec(memory_space=pltpu.HBM)
    dma = pltpu.SemaphoreType.DMA
    wide = d * 4 * wl // LANES
    return pl.pallas_call(
        functools.partial(pair_kernel, n),
        out_shape=jax.ShapeDtypeStruct((rows, d), bf16),
        in_specs=[hbm, hbm, hbm, hbm, hbm, hbm, hbm, smem, smem],
        out_specs=vmem,
        scratch_shapes=[
            pltpu.VMEM((rows, d), bf16),
            pltpu.VMEM((layers, wide, LANES), bf16),
            pltpu.VMEM((wide, LANES), f32),
            pltpu.VMEM((layers, d, 4 * wl), bf16),
            pltpu.VMEM(w_out.shape, bf16),
            pltpu.VMEM((layers, heads, rab_table.shape[1]), f32),
            pltpu.VMEM((1, hist_dev), jnp.int32),
            pltpu.VMEM((layers, hist_dev, wl), bf16),
            pltpu.VMEM((layers, hist_dev, wl), bf16),
            pltpu.VMEM((layers, heads, hist_dev, LANES), bf16),
            pltpu.VMEM((LANES, layers * heads * LANES), bf16),
            pltpu.VMEM((hist_dev, LANES), bf16),
            pltpu.VMEM(w_out.shape, bf16),
            pltpu.VMEM((layers, HALVES, n * half, wl), bf16),
            pltpu.VMEM((heads, 2 * half, LANES), bf16),
            pltpu.VMEM((layers, HALVES, n * half, wl), bf16),
            pltpu.VMEM((layers, HALVES, n, half, wl), bf16),
            pltpu.VMEM((rows, d), f32),
            pltpu.VMEM((rows, d), bf16),
            pltpu.VMEM((rows, wl), bf16),
            pltpu.VMEM((rows, wl), f32),
            pltpu.VMEM((layers, HALVES, half, wl), f32),
            pltpu.VMEM((layers, HALVES, half, wl), f32),
            pltpu.VMEM((layers, HALVES, half, wl), bf16),
            pltpu.VMEM((layers, HALVES, half, wl), bf16),
            dma((6 + layers,)),
            dma((layers, HALVES, n)),
            dma((layers, HALVES, n)),
            dma((layers, HALVES, n)),
            dma((layers, HALVES, n)),
            dma((layers, HALVES)),
            dma((layers, HALVES)),
            dma((layers, HALVES)),
            dma((layers, HALVES)),
            dma,
            dma,
        ],
        compiler_params=pltpu.CompilerParams(
            collective_id=1, has_side_effects=True, vmem_limit_bytes=60 * 1024 * 1024
        ),
    )(
        candidates,
        w_in.reshape(layers, d, 4, wl // LANES, LANES)
        .transpose(0, 1, 3, 2, 4)
        .reshape(layers, wide, LANES),
        key_cache,
        value_cache,
        w_out,
        rab_table.transpose(0, 2, 1),
        hist_bucket.reshape(1, hist_dev),
        hist_len,
        visible,
    )


def in_pairs(mesh):
    n = mesh.shape["hist"]
    if n != 8:
        return False
    index = [slice(None) if name == "hist" else 0 for name in mesh.axis_names]
    spots = [getattr(device, "coords", None) for device in mesh.devices[tuple(index)][:3]]
    if any(spot is None for spot in spots):
        return False
    apart = [sum(abs(a - b) for a, b in zip(spots[0], spot)) for spot in spots[1:]]
    return apart == [1, 1]


def solution(mesh):
    placed = (
        P(("users", "hist"), None),
        P(None, ("users", "hist"), "head"),
        P(None, ("users", "hist"), "head"),
        P(None, None, None, "head"),
        P(None, "head", None),
        P(None, None, "head"),
        P(("users", "hist")),
        P(("users", "hist")),
        P(None, ("users", "hist")),
    )
    chosen = pair_shards if in_pairs(mesh) else shards
    return jax.shard_map(
        functools.partial(chosen, mesh.shape["hist"]),
        mesh=mesh,
        in_specs=placed,
        out_specs=P(("users", "hist"), None),
        check_vma=False,
    )
```

```python
import functools

import jax
import jax.numpy as jnp
from jax import lax
from jax.experimental import pallas as pl
from jax.experimental.pallas import tpu as pltpu
from jax.sharding import PartitionSpec as P

DH = 64
BLOCK = 256
LANES = 128
PER = LANES // DH
GROUP_ROWS = 256
KEY_CHUNK = 2048
BIG = 16384.0
MESH = pl.DeviceIdType.MESH
HALVES = 2
SENDS = ((3, 0), (3, 1), (0, 1), (1, 0), (1, 1))
GATHER = ((3, 0), (3, 1), (1, 0), (1, 1), (2, 0), (2, 1), (0, 1))
ORDER = ((1, 3, 0, 2, 2, 1, 3, 0), (1, 3, 0, 2, 1, 3, 0, 2))
ORDERS = [sum(dz << (2 * t) for t, dz in enumerate(order)) for order in ORDER]
FORWARD = (2, 3)
SUM_A = (7, 7)
SUM_B = 0
END_B = 0

epsilon = 1e-05


def silu(v):
    return v / (1.0 + jnp.exp(-v))


def dot(a, b):
    return jnp.dot(a, b, preferred_element_type=jnp.float32)


def kernel(
    n,
    cand_hbm,
    w_hbm,
    key_hbm,
    val_hbm,
    wo_hbm,
    rab_hbm,
    bucket_hbm,
    hlen,
    vis,
    out,
    cand,
    raw,
    wide,
    w_in,
    w_out,
    rab,
    bucket,
    keys,
    vals,
    kaug,
    table,
    events,
    w_other,
    qall,
    qaug,
    part,
    parts_in,
    acc,
    att_send,
    att_in,
    gate_send,
    gate_in,
    load_sem,
    q_send,
    q_recv,
    p_send,
    p_recv,
    h_send,
    h_recv,
):
    me = lax.axis_index("hist")
    other = 1 - lax.axis_index("head")
    layers, hist_dev, wl = key_hbm.shape
    rows, d = cand.shape
    heads = wl // DH
    parts_w = 4
    pairs = wl // LANES
    nb = rab.shape[2]
    micro, blocks = vis.shape
    total = n * rows
    micro_rows = total // micro
    group_rows = min(GROUP_ROWS, total)
    per_group = group_rows // rows
    groups = n // per_group
    key_chunk = min(KEY_CHUNK, hist_dev)

    load_k = pltpu.make_async_copy(key_hbm, keys, load_sem.at[0])
    load_v = pltpu.make_async_copy(val_hbm, vals, load_sem.at[1])
    load_c = pltpu.make_async_copy(cand_hbm, cand, load_sem.at[2])
    load_w = [
        pltpu.make_async_copy(w_hbm.at[l], raw.at[l], load_sem.at[3 + l]) for l in range(layers)
    ]
    load_o = pltpu.make_async_copy(wo_hbm, w_out, load_sem.at[3 + layers])
    load_r = pltpu.make_async_copy(rab_hbm, rab, load_sem.at[4 + layers])
    load_b = pltpu.make_async_copy(bucket_hbm, bucket, load_sem.at[5 + layers])
    load_c.start()
    load_w[0].start()
    load_b.start()
    load_r.start()
    load_k.start()
    load_o.start()
    load_v.start()
    for copy in load_w[1:]:
        copy.start()

    barrier = pltpu.get_barrier_semaphore()
    for j in range(1, n):
        pl.semaphore_signal(
            barrier, inc=1, device_id={"hist": lax.rem(me + j, n)}, device_id_type=MESH
        )
    pl.semaphore_signal(barrier, inc=1, device_id={"head": other}, device_id_type=MESH)

    def to_head(src, dst, index):
        return pltpu.make_async_remote_copy(
            src_ref=src,
            dst_ref=dst,
            send_sem=h_send.at[index],
            recv_sem=h_recv.at[index],
            device_id={"head": other},
            device_id_type=MESH,
        )

    def unpack_w(l):
        halves = wl // LANES
        step = halves * parts_w
        wide[...] = raw[l].astype(jnp.float32)
        for i in range(parts_w):
            for c in range(halves):
                start = i * wl + c * LANES
                w_in[:, start : start + LANES] = wide[
                    pl.ds(c * parts_w + i, d, stride=step), :
                ].astype(jnp.bfloat16)

    def row_of(s):
        return pl.ds(pl.multiple_of(s * rows, rows), rows)

    def q_copy(l, s, owner):
        return pltpu.make_async_remote_copy(
            src_ref=qall.at[l, row_of(owner)],
            dst_ref=qall.at[l, row_of(owner)],
            send_sem=q_send.at[l, s],
            recv_sem=q_recv.at[l, owner],
            device_id={"hist": s},
            device_id_type=MESH,
        )

    def p_copy(l, s, owner):
        return pltpu.make_async_remote_copy(
            src_ref=part.at[l, row_of(s)],
            dst_ref=parts_in.at[l, owner],
            send_sem=p_send.at[l, s],
            recv_sem=p_recv.at[l, owner],
            device_id={"hist": s},
            device_id_type=MESH,
        )

    def build_keys():
        lane = lax.broadcasted_iota(jnp.int32, (LANES, LANES), 1)
        lane8 = lax.broadcasted_iota(jnp.int32, (blocks, LANES), 1)
        row8 = lax.broadcasted_iota(jnp.int32, (blocks, LANES), 0)
        base_of = (DH, 0)
        seen = []
        gone = []
        for base in base_of:
            held = jnp.zeros((blocks, LANES), jnp.float32)
            for m in range(micro):
                column = jnp.zeros((blocks, LANES), jnp.float32)
                for b in range(blocks):
                    value = (vis[m, b] - 1).astype(jnp.float32) * BIG
                    column = jnp.where(row8 == b, value, column)
                held = jnp.where(lane8 == base + 2 + m, column, held)
            seen.append(held)
            is_micro = (lane8 >= base + 2) & (lane8 < base + 2 + micro)
            gone.append(jnp.where(is_micro & (row8 == 0), -BIG, 0.0))
        for l in range(layers):
            flat = jnp.concatenate([rab[l], jnp.zeros((heads, LANES - nb), jnp.float32)], axis=1)
            flat = jnp.concatenate([flat, jnp.zeros((8 - heads, LANES), jnp.float32)], axis=0)
            upright = flat.T
            for h in range(heads):
                base = base_of[h % PER]
                half = upright[:nb, h : h + 1] * 0.5
                high = half.astype(jnp.bfloat16).astype(jnp.float32)
                low = half - high
                lane_nb = lane[:nb]
                bias = jnp.where(lane_nb == base, high, jnp.where(lane_nb == base + 1, low, 0.0))
                fill = jnp.zeros((LANES - nb - 2 * blocks, LANES), jnp.float32)
                whole = jnp.concatenate([bias, seen[h % PER], gone[h % PER], fill], axis=0)
                start = (l * heads + h) * LANES
                table[:, start : start + LANES] = whole.astype(jnp.bfloat16)

        row = lax.broadcasted_iota(jnp.int32, (LANES, key_chunk), 0)
        spot = lax.broadcasted_iota(jnp.int32, (LANES, key_chunk), 1)
        lane_k = lax.broadcasted_iota(jnp.int32, (key_chunk, LANES), 1)
        length = hlen[0]
        for c in range(hist_dev // key_chunk):
            span = slice(c * key_chunk, (c + 1) * key_chunk)
            place = spot + c * key_chunk
            here = (
                (row == bucket[:, span])
                | (row == nb + place // BLOCK)
                | ((row == nb + blocks) & (place >= length))
            )
            events[span, :] = jnp.where(here, 1.0, 0.0).T.astype(jnp.bfloat16)
        load_k.wait()

        def chunk(c, carry):
            span = pl.ds(pl.multiple_of(c * key_chunk, key_chunk), key_chunk)
            spread = events[span, :]
            for l in range(layers):
                for h in range(heads):
                    start = (l * heads + h) * LANES
                    extra = dot(spread, table[:, start : start + LANES])
                    p = h // PER
                    tile = keys[l, span, p * LANES : (p + 1) * LANES].astype(jnp.float32)
                    mine = (lane_k < DH) if h % PER == 0 else (lane_k >= DH)
                    kaug[l, h, span, :] = jnp.where(mine, tile, extra).astype(jnp.bfloat16)
            return carry

        lax.fori_loop(0, hist_dev // key_chunk, chunk, 0)

    lane_q = lax.broadcasted_iota(jnp.int32, (group_rows, LANES), 1)
    row_q = lax.broadcasted_iota(jnp.int32, (group_rows, LANES), 0)
    lane_a = lax.broadcasted_iota(jnp.int32, (group_rows, LANES), 1)

    def attend(l, g):
        span = pl.ds(pl.multiple_of(g * group_rows, group_rows), group_rows)
        which = (row_q + g * group_rows) // micro_rows
        for h in range(heads):
            p = h // PER
            base = DH if h % PER == 0 else 0
            tile = qall[l, span, p * LANES : (p + 1) * LANES].astype(jnp.float32)
            ones = (lane_q == base) | (lane_q == base + 1) | (lane_q == base + 2 + which)
            mine = (lane_q < DH) if h % PER == 0 else (lane_q >= DH)
            qaug[h] = jnp.where(mine, tile, jnp.where(ones, 1.0, 0.0)).astype(jnp.bfloat16)
        acc[...] = jnp.zeros_like(acc)

        def chunk(c, carry):
            keys_at = pl.ds(pl.multiple_of(c * key_chunk, key_chunk), key_chunk)
            for p in range(pairs):
                value = vals[l, keys_at, p * LANES : (p + 1) * LANES]
                found = []
                for e in range(PER):
                    h = p * PER + e
                    y = lax.dot_general(
                        qaug[h],
                        kaug[l, h, keys_at, :],
                        (((1,), (1,)), ((), ())),
                        preferred_element_type=jnp.float32,
                    ).astype(jnp.bfloat16)
                    weight = y * (jnp.tanh(y) + 1.0)
                    found.append(dot(weight, value))
                acc[:, p * LANES : (p + 1) * LANES] += jnp.where(lane_a < DH, found[0], found[1])
            return carry

        lax.fori_loop(0, hist_dev // key_chunk, chunk, 0)
        part[l, span, :] = acc[...].astype(jnp.bfloat16)

    block_row = lax.broadcasted_iota(jnp.int32, (wl, wl), 0) // DH
    block_col = lax.broadcasted_iota(jnp.int32, (wl, wl), 1) // DH
    same_head = jnp.where(block_row == block_col, 1.0, 0.0).astype(jnp.bfloat16)

    load_c.wait()
    stream = cand[...].astype(jnp.float32)
    for l in range(layers):
        load_w[l].wait()
        unpack_w(l)
        average = jnp.mean(stream, axis=-1, keepdims=True)
        centred = stream - average
        variance = jnp.mean(centred * centred, axis=-1, keepdims=True)
        normed = (centred * lax.rsqrt(variance + epsilon)).astype(jnp.bfloat16)

        def project(i):
            return silu(dot(normed, w_in[:, i * wl : (i + 1) * wl])).astype(jnp.bfloat16)

        queries = project(0).astype(jnp.float32)
        qall[l, row_of(me), :] = (queries * (0.5 * DH**-0.5)).astype(jnp.bfloat16)
        if l == 0:
            pl.semaphore_wait(barrier, n)
        for j in range(1, n):
            q_copy(l, lax.rem(me + j, n), me).start()
        keys_new = project(1).astype(jnp.float32)
        values_new = project(2).astype(jnp.float32)
        gates = project(3)
        gate_send[l] = gates
        gate_copy = to_head(gate_send.at[l], gate_in.at[l], 2 * l)
        gate_copy.start()
        if l == 0:
            load_o.wait()
            w_copy = to_head(w_out, w_other, 2 * layers)
            w_copy.start()
        product = queries * keys_new
        high = product.astype(jnp.bfloat16)
        low = (product - high.astype(jnp.float32)).astype(jnp.bfloat16)
        own_score = dot(high, same_head) + dot(low, same_head)
        own = silu(own_score * (DH**-0.5)) * values_new
        if l == 0:
            load_r.wait()
            load_b.wait()
            build_keys()
            load_v.wait()

        def group(t, carry):
            g = lax.rem(me // per_group + t, groups)
            for i in range(per_group):
                s = g * per_group + i

                @pl.when(s != me)
                def _():
                    q_copy(l, s, s).wait_recv()

            attend(l, g)
            for i in range(per_group):
                s = g * per_group + i

                @pl.when(s != me)
                def _():
                    p_copy(l, s, me).start()

            return carry

        lax.fori_loop(0, groups, group, 0)
        history = part[l, row_of(me), :].astype(jnp.float32)
        for j in range(1, n):
            s = lax.rem(me + j, n)
            p_copy(l, s, s).wait_recv()
            history = history + parts_in[l, s].astype(jnp.float32)
        attended = history + own
        att_send[l] = attended
        att_copy = to_head(att_send.at[l], att_in.at[l], 2 * l + 1)
        att_copy.start()
        if l == 0:
            w_copy.wait_recv()
        gate_copy.wait_recv()
        att_copy.wait_recv()
        theirs = att_in[l]
        width = 2 * wl
        mean = (
            jnp.sum(attended, axis=-1, keepdims=True) + jnp.sum(theirs, axis=-1, keepdims=True)
        ) / width
        square = (
            jnp.sum(attended * attended, axis=-1, keepdims=True)
            + jnp.sum(theirs * theirs, axis=-1, keepdims=True)
        ) / width
        rstd = lax.rsqrt(square - mean * mean + epsilon)
        gated = ((attended - mean) * rstd * gates.astype(jnp.float32)).astype(jnp.bfloat16)
        gated_other = ((theirs - mean) * rstd * gate_in[l].astype(jnp.float32)).astype(
            jnp.bfloat16
        )
        stream = stream + (dot(gated, w_out[l]) + dot(gated_other, w_other[l]))
        gate_copy.wait_send()
        att_copy.wait_send()
        if l == 0:
            w_copy.wait_send()
        for j in range(1, n):
            s = lax.rem(me + j, n)
            q_copy(l, s, me).wait_send()
            p_copy(l, s, me).wait_send()
    out[...] = stream.astype(out.dtype)


def shards(
    n, candidates, key_cache, value_cache, w_in, w_out, rab_table, hist_len, hist_bucket, visible
):
    layers, hist_dev, wl = key_cache.shape
    rows, d = candidates.shape
    heads = wl // DH
    total = n * rows
    group_rows = min(GROUP_ROWS, total)
    bf16, f32 = jnp.bfloat16, jnp.float32
    vmem = pl.BlockSpec(memory_space=pltpu.VMEM)
    smem = pl.BlockSpec(memory_space=pltpu.SMEM)
    hbm = pl.BlockSpec(memory_space=pltpu.HBM)
    dma = pltpu.SemaphoreType.DMA
    return pl.pallas_call(
        functools.partial(kernel, n),
        out_shape=jax.ShapeDtypeStruct((rows, d), bf16),
        in_specs=[hbm, hbm, hbm, hbm, hbm, hbm, hbm, smem, smem],
        out_specs=vmem,
        scratch_shapes=[
            pltpu.VMEM((rows, d), bf16),
            pltpu.VMEM((layers, d * 4 * wl // LANES, LANES), bf16),
            pltpu.VMEM((d * 4 * wl // LANES, LANES), f32),
            pltpu.VMEM((d, 4 * wl), bf16),
            pltpu.VMEM(w_out.shape, bf16),
            pltpu.VMEM((layers, heads, rab_table.shape[1]), f32),
            pltpu.VMEM((1, hist_dev), jnp.int32),
            pltpu.VMEM((layers, hist_dev, wl), bf16),
            pltpu.VMEM((layers, hist_dev, wl), bf16),
            pltpu.VMEM((layers, heads, hist_dev, LANES), bf16),
            pltpu.VMEM((LANES, layers * heads * LANES), bf16),
            pltpu.VMEM((hist_dev, LANES), bf16),
            pltpu.VMEM(w_out.shape, bf16),
            pltpu.VMEM((layers, total, wl), bf16),
            pltpu.VMEM((heads, group_rows, LANES), bf16),
            pltpu.VMEM((layers, total, wl), bf16),
            pltpu.VMEM((layers, n, rows, wl), bf16),
            pltpu.VMEM((group_rows, wl), f32),
            pltpu.VMEM((layers, rows, wl), f32),
            pltpu.VMEM((layers, rows, wl), f32),
            pltpu.VMEM((layers, rows, wl), bf16),
            pltpu.VMEM((layers, rows, wl), bf16),
            dma((6 + layers,)),
            dma((layers, n)),
            dma((layers, n)),
            dma((layers, n)),
            dma((layers, n)),
            dma((2 * layers + 1,)),
            dma((2 * layers + 1,)),
        ],
        compiler_params=pltpu.CompilerParams(
            collective_id=0, has_side_effects=True, vmem_limit_bytes=60 * 1024 * 1024
        ),
    )(
        candidates,
        w_in.reshape(layers, d, 4, wl // LANES, LANES)
        .transpose(0, 1, 3, 2, 4)
        .reshape(layers, d * 4 * wl // LANES, LANES),
        key_cache,
        value_cache,
        w_out,
        rab_table.transpose(0, 2, 1),
        hist_bucket.reshape(1, hist_dev),
        hist_len,
        visible,
    )


def pair_kernel(
    n,
    cand_hbm,
    w_hbm,
    key_hbm,
    val_hbm,
    wo_hbm,
    rab_hbm,
    bucket_hbm,
    hlen,
    vis,
    out,
    cand,
    raw,
    wide,
    w_in,
    w_out,
    rab,
    bucket,
    keys,
    vals,
    kaug,
    table,
    events,
    w_other,
    qall,
    qaug,
    part,
    parts_in,
    stream,
    normed,
    q_own,
    own,
    att_send,
    att_in,
    gate_send,
    gate_in,
    load_sem,
    q_send,
    q_recv,
    p_send,
    p_recv,
    a_send,
    a_recv,
    g_send,
    g_recv,
    w_send,
    w_recv,
):
    me = lax.axis_index("hist")
    other = 1 - lax.axis_index("head")
    layers, hist_dev, wl = key_hbm.shape
    rows, d = cand.shape
    heads = wl // DH
    pairs = wl // LANES
    nb = rab.shape[2]
    micro, blocks = vis.shape
    micro_rows = n * rows // micro
    half = rows // HALVES
    pair = 2 * half
    outer = n // 2
    calls = HALVES * outer
    line, side = me // 2, lax.rem(me, 2)
    beside = line * 2 + 1 - side

    load_c = pltpu.make_async_copy(cand_hbm, cand, load_sem.at[0])
    load_w = [
        pltpu.make_async_copy(w_hbm.at[l], raw.at[l], load_sem.at[6 + l]) for l in range(layers)
    ]
    load_k = pltpu.make_async_copy(key_hbm, keys, load_sem.at[1])
    load_v = pltpu.make_async_copy(val_hbm, vals, load_sem.at[2])
    load_o = pltpu.make_async_copy(wo_hbm, w_out, load_sem.at[3])
    load_r = pltpu.make_async_copy(rab_hbm, rab, load_sem.at[4])
    load_b = pltpu.make_async_copy(bucket_hbm, bucket, load_sem.at[5])
    load_c.start()
    load_w[0].start()

    barrier = pltpu.get_barrier_semaphore()
    for j in range(1, n):
        pl.semaphore_signal(
            barrier, inc=1, device_id={"hist": lax.rem(me + j, n)}, device_id_type=MESH
        )
    pl.semaphore_signal(barrier, inc=1, device_id={"head": other}, device_id_type=MESH)

    load_b.start()
    load_r.start()
    load_k.start()
    load_o.start()
    load_v.start()
    for copy in load_w[1:]:
        copy.start()

    def to_head(src, dst, send, recv):
        return pltpu.make_async_remote_copy(
            src_ref=src,
            dst_ref=dst,
            send_sem=send,
            recv_sem=recv,
            device_id={"head": other},
            device_id_type=MESH,
        )

    w_copy = to_head(w_out, w_other, w_send, w_recv)

    def att_copy(l, f):
        return to_head(att_send.at[l, f], att_in.at[l, f], a_send.at[l, f], a_recv.at[l, f])

    def gate_copy(l, f):
        return to_head(gate_send.at[l, f], gate_in.at[l, f], g_send.at[l, f], g_recv.at[l, f])

    def unit(s):
        return pl.ds(pl.multiple_of(s * half, half), half)

    def unit_pair(z):
        return pl.ds(pl.multiple_of(z * pair, pair), pair)

    def near(dz, dy):
        return lax.rem(line + dz, outer) * 2 + lax.rem(side + dy, 2)

    def q_copy(l, f, s, owner):
        return pltpu.make_async_remote_copy(
            src_ref=qall.at[l, f, unit(owner)],
            dst_ref=qall.at[l, f, unit(owner)],
            send_sem=q_send.at[l, f, s],
            recv_sem=q_recv.at[l, f, owner],
            device_id={"hist": s},
            device_id_type=MESH,
        )

    def relay_copy(l, f, z):
        return pltpu.make_async_remote_copy(
            src_ref=qall.at[l, f, unit_pair(z)],
            dst_ref=qall.at[l, f, unit_pair(z)],
            send_sem=q_send.at[l, f, me],
            recv_sem=q_recv.at[l, f, 2 * z],
            device_id={"hist": near(outer - 1, 0)},
            device_id_type=MESH,
        )

    def p_copy(l, f, s, owner):
        return pltpu.make_async_remote_copy(
            src_ref=part.at[l, f, unit(s)],
            dst_ref=parts_in.at[l, f, owner],
            send_sem=p_send.at[l, f, s],
            recv_sem=p_recv.at[l, f, owner],
            device_id={"hist": s},
            device_id_type=MESH,
        )

    def send_q(l, f):
        for dz, dy in SENDS:
            q_copy(l, f, near(dz, dy), me).start()

    def unpack_w(l, first, last):
        halves = wl // LANES
        step = halves * 4
        if first == 0:
            load_w[l].wait()
            wide[...] = raw[l].astype(jnp.float32)
        for i in range(first, last):
            for c in range(halves):
                start = i * wl + c * LANES
                w_in[l, :, start : start + LANES] = wide[
                    pl.ds(c * 4 + i, d, stride=step), :
                ].astype(jnp.bfloat16)

    def build_tables():
        lane8 = lax.broadcasted_iota(jnp.int32, (blocks, LANES), 1)
        row8 = lax.broadcasted_iota(jnp.int32, (blocks, LANES), 0)
        lane_nb = lax.broadcasted_iota(jnp.int32, (nb, LANES), 1)
        base_of = (DH, 0)
        seen = []
        gone = []
        for base in base_of:
            held = jnp.zeros((blocks, LANES), jnp.float32)
            for m in range(micro):
                column = jnp.zeros((blocks, LANES), jnp.float32)
                for b in range(blocks):
                    value = (vis[m, b] - 1).astype(jnp.float32) * BIG
                    column = jnp.where(row8 == b, value, column)
                held = jnp.where(lane8 == base + 2 + m, column, held)
            seen.append(held)
            is_micro = (lane8 >= base + 2) & (lane8 < base + 2 + micro)
            gone.append(jnp.where(is_micro & (row8 == 0), -BIG, 0.0))
        load_r.wait()
        for l in range(layers):
            flat = jnp.concatenate([rab[l], jnp.zeros((heads, LANES - nb), jnp.float32)], axis=1)
            flat = jnp.concatenate([flat, jnp.zeros((8 - heads, LANES), jnp.float32)], axis=0)
            upright = flat.T
            for h in range(heads):
                base = base_of[h % PER]
                score = upright[:nb, h : h + 1] * 0.5
                high = score.astype(jnp.bfloat16).astype(jnp.float32)
                low = score - high
                bias = jnp.where(lane_nb == base, high, jnp.where(lane_nb == base + 1, low, 0.0))
                fill = jnp.zeros((LANES - nb - 2 * blocks, LANES), jnp.float32)
                whole = jnp.concatenate([bias, seen[h % PER], gone[h % PER], fill], axis=0)
                start = (l * heads + h) * LANES
                table[:, start : start + LANES] = whole.astype(jnp.bfloat16)

        row = lax.broadcasted_iota(jnp.int32, (LANES, hist_dev), 0)
        place = lax.broadcasted_iota(jnp.int32, (LANES, hist_dev), 1)
        load_b.wait()
        here = (
            (row == bucket[...])
            | (row == nb + place // BLOCK)
            | ((row == nb + blocks) & (place >= hlen[0]))
        )
        events[...] = jnp.where(here, 1.0, 0.0).T.astype(jnp.bfloat16)

    def augment_keys(l):
        lane_k = lax.broadcasted_iota(jnp.int32, (hist_dev, LANES), 1)
        for h in range(heads):
            start = (l * heads + h) * LANES
            extra = dot(events[...], table[:, start : start + LANES])
            p = h // PER
            tile = keys[l, :, p * LANES : (p + 1) * LANES].astype(jnp.float32)
            mine = (lane_k < DH) if h % PER == 0 else (lane_k >= DH)
            kaug[l, h] = jnp.where(mine, tile, extra).astype(jnp.bfloat16)

    lane_q = lax.broadcasted_iota(jnp.int32, (pair, LANES), 1)
    row_q = lax.broadcasted_iota(jnp.int32, (pair, LANES), 0)

    def attend(l, f, z):
        span = unit_pair(z)
        place = (z * 2 + row_q // half) * rows + f * half + row_q % half
        which = place // micro_rows
        for h in range(heads):
            p = h // PER
            base = DH if h % PER == 0 else 0
            tile = qall[l, f, span, p * LANES : (p + 1) * LANES].astype(jnp.float32)
            ones = (lane_q == base) | (lane_q == base + 1) | (lane_q == base + 2 + which)
            mine = (lane_q < DH) if h % PER == 0 else (lane_q >= DH)
            qaug[h] = jnp.where(mine, tile, jnp.where(ones, 1.0, 0.0)).astype(jnp.bfloat16)
        for p in range(pairs):
            value = vals[l, :, p * LANES : (p + 1) * LANES]
            found = []
            for e in range(PER):
                h = p * PER + e
                y = lax.dot_general(
                    qaug[h],
                    kaug[l, h],
                    (((1,), (1,)), ((), ())),
                    preferred_element_type=jnp.float32,
                ).astype(jnp.bfloat16)
                weight = y * (jnp.tanh(y) + 1.0)
                found.append(dot(weight, value))
            both = jnp.where(lane_q < DH, found[0], found[1])
            part[l, f, span, p * LANES : (p + 1) * LANES] = both.astype(jnp.bfloat16)

    block_row = lax.broadcasted_iota(jnp.int32, (wl, wl), 0) // DH
    block_col = lax.broadcasted_iota(jnp.int32, (wl, wl), 1) // DH
    same_head = jnp.where(block_row == block_col, 1.0, 0.0).astype(jnp.bfloat16)

    def normalize(l, first, last):
        mine = slice(first * half, last * half)
        x = stream[mine]
        centred = x - jnp.mean(x, axis=-1, keepdims=True)
        variance = jnp.mean(centred * centred, axis=-1, keepdims=True)
        normed[mine] = (centred * lax.rsqrt(variance + epsilon)).astype(jnp.bfloat16)

    def make_queries(l, first, last):
        mine = slice(first * half, last * half)
        queries = silu(dot(normed[mine], w_in[l, :, :wl])).astype(jnp.bfloat16)
        scaled = (queries.astype(jnp.float32) * (0.5 * DH**-0.5)).astype(jnp.bfloat16)
        for f in range(first, last):
            qall[l, f, unit(me)] = scaled[(f - first) * half : (f - first + 1) * half]
        q_own[mine] = queries

    def make_rest(l, first, last):
        mine = slice(first * half, last * half)

        def project(i):
            sums = dot(normed[mine], w_in[l, :, i * wl : (i + 1) * wl])
            return silu(sums).astype(jnp.bfloat16)

        gates = project(3)
        for f in range(first, last):
            gate_send[l, f] = gates[(f - first) * half : (f - first + 1) * half]
            gate_copy(l, f).start()
        keys_new = project(1).astype(jnp.float32)
        values_new = project(2).astype(jnp.float32)
        product = q_own[mine].astype(jnp.float32) * keys_new
        high = product.astype(jnp.bfloat16)
        low = (product - high.astype(jnp.float32)).astype(jnp.bfloat16)
        own_score = dot(high, same_head) + dot(low, same_head)
        own[mine] = silu(own_score * (DH**-0.5)) * values_new

    def add_parts(l, f):
        history = part[l, f, unit(me), :].astype(jnp.float32)
        for dz, dy in GATHER:
            s = near(dz, dy)
            p_copy(l, f, s, s).wait_recv()
            history = history + parts_in[l, f, s].astype(jnp.float32)
        att_send[l, f] = history + own[f * half : (f + 1) * half]
        att_copy(l, f).start()

    def finish(l, f):
        mine = slice(f * half, (f + 1) * half)
        if l == 0 and f == 0:
            w_copy.wait_recv()
        gate_copy(l, f).wait_recv()
        att_copy(l, f).wait_recv()
        attended, theirs = att_send[l, f], att_in[l, f]
        width = 2 * wl
        mean = (
            jnp.sum(attended, axis=-1, keepdims=True) + jnp.sum(theirs, axis=-1, keepdims=True)
        ) / width
        square = (
            jnp.sum(attended * attended, axis=-1, keepdims=True)
            + jnp.sum(theirs * theirs, axis=-1, keepdims=True)
        ) / width
        rstd = lax.rsqrt(square - mean * mean + epsilon)
        gates, gates_other = gate_send[l, f], gate_in[l, f]
        gated = ((attended - mean) * rstd * gates.astype(jnp.float32)).astype(jnp.bfloat16)
        gated_other = ((theirs - mean) * rstd * gates_other.astype(jnp.float32)).astype(
            jnp.bfloat16
        )
        x = stream[mine] + (dot(gated, w_out[l]) + dot(gated_other, w_other[l]))
        if l + 1 < layers:
            stream[mine] = x
        else:
            out[mine] = x.astype(out.dtype)

    load_c.wait()
    stream[...] = cand[...].astype(jnp.float32)
    normalize(0, 0, HALVES)
    unpack_w(0, 0, 1)
    make_queries(0, 0, HALVES)

    def prepare():
        build_tables()
        load_k.wait()
        augment_keys(0)
        for l in range(1, layers):
            unpack_w(l, 0, 4)

    pl.semaphore_wait(barrier, n)
    for f in range(HALVES):
        send_q(0, f)
    unpack_w(0, 1, 4)
    make_rest(0, 0, HALVES)
    load_o.wait()
    w_copy.start()
    prepare()
    load_v.wait()

    def call(t, carry):
        l, f = t // calls, (t // outer) % HALVES
        for late in range(layers):
            first = late * calls

            if SUM_A[min(late, 1)] < calls:

                @pl.when(t == first + SUM_A[min(late, 1)])
                def _(late=late):
                    add_parts(late, 0)

            if late + 1 < layers:

                @pl.when(t == first + calls)
                def _(late=late):
                    if SUM_A[min(late, 1)] == calls:
                        add_parts(late, 0)
                    finish(late, 0)
                    normalize(late + 1, 0, 1)
                    make_queries(late + 1, 0, 1)
                    send_q(late + 1, 0)
                    make_rest(late + 1, 0, 1)
                    augment_keys(late + 1)

                @pl.when(t == first + calls + SUM_B)
                def _(late=late):
                    add_parts(late, 1)

                @pl.when(t == first + calls + END_B)
                def _(late=late):
                    finish(late, 1)
                    normalize(late + 1, 1, 2)
                    make_queries(late + 1, 1, 2)
                    send_q(late + 1, 1)
                    make_rest(late + 1, 1, 2)

        kind = jnp.minimum(l, 1)
        code = ORDERS[0] + kind * (ORDERS[1] - ORDERS[0])
        dz = lax.shift_right_logical(code, 2 * (t % calls)) & 3
        z = lax.rem(line + dz, outer)
        @pl.when(dz == 0)
        def _():
            q_copy(l, f, beside, beside).wait_recv()

        @pl.when(t % calls == FORWARD[0] + kind * (FORWARD[1] - FORWARD[0]))
        def _():
            after = lax.rem(line + 1, outer)
            for i in range(2):
                q_copy(l, 1, 2 * after + i, 2 * after + i).wait_recv()
            relay_copy(l, 1, after).start()

        @pl.when(dz == 2)
        def _():
            relay_copy(l, f, z).wait_recv()

        @pl.when((dz == 3) | ((dz == 1) & (f == 0)))
        def _():
            for i in range(2):
                q_copy(l, f, 2 * z + i, 2 * z + i).wait_recv()

        @pl.when((dz == 1) & (f == 0))
        def _():
            relay_copy(l, f, z).start()

        attend(l, f, z)
        for i in range(2):
            s = 2 * z + i

            @pl.when(s != me)
            def _(s=s):
                p_copy(l, f, s, me).start()

        return carry

    lax.fori_loop(0, layers * calls, call, 0)
    if SUM_A[min(layers - 1, 1)] == calls:
        add_parts(layers - 1, 0)
    finish(layers - 1, 0)
    add_parts(layers - 1, 1)
    finish(layers - 1, 1)

    w_copy.wait_send()
    for l in range(layers):
        for f in range(HALVES):
            att_copy(l, f).wait_send()
            gate_copy(l, f).wait_send()
            for dz, dy in SENDS:
                q_copy(l, f, near(dz, dy), me).wait_send()
            relay_copy(l, f, lax.rem(line + 1, outer)).wait_send()
            for j in range(1, n):
                p_copy(l, f, lax.rem(me + j, n), me).wait_send()


def pair_shards(
    n, candidates, key_cache, value_cache, w_in, w_out, rab_table, hist_len, hist_bucket, visible
):
    layers, hist_dev, wl = key_cache.shape
    rows, d = candidates.shape
    heads = wl // DH
    half = rows // HALVES
    bf16, f32 = jnp.bfloat16, jnp.float32
    vmem = pl.BlockSpec(memory_space=pltpu.VMEM)
    smem = pl.BlockSpec(memory_space=pltpu.SMEM)
    hbm = pl.BlockSpec(memory_space=pltpu.HBM)
    dma = pltpu.SemaphoreType.DMA
    wide = d * 4 * wl // LANES
    return pl.pallas_call(
        functools.partial(pair_kernel, n),
        out_shape=jax.ShapeDtypeStruct((rows, d), bf16),
        in_specs=[hbm, hbm, hbm, hbm, hbm, hbm, hbm, smem, smem],
        out_specs=vmem,
        scratch_shapes=[
            pltpu.VMEM((rows, d), bf16),
            pltpu.VMEM((layers, wide, LANES), bf16),
            pltpu.VMEM((wide, LANES), f32),
            pltpu.VMEM((layers, d, 4 * wl), bf16),
            pltpu.VMEM(w_out.shape, bf16),
            pltpu.VMEM((layers, heads, rab_table.shape[1]), f32),
            pltpu.VMEM((1, hist_dev), jnp.int32),
            pltpu.VMEM((layers, hist_dev, wl), bf16),
            pltpu.VMEM((layers, hist_dev, wl), bf16),
            pltpu.VMEM((layers, heads, hist_dev, LANES), bf16),
            pltpu.VMEM((LANES, layers * heads * LANES), bf16),
            pltpu.VMEM((hist_dev, LANES), bf16),
            pltpu.VMEM(w_out.shape, bf16),
            pltpu.VMEM((layers, HALVES, n * half, wl), bf16),
            pltpu.VMEM((heads, 2 * half, LANES), bf16),
            pltpu.VMEM((layers, HALVES, n * half, wl), bf16),
            pltpu.VMEM((layers, HALVES, n, half, wl), bf16),
            pltpu.VMEM((rows, d), f32),
            pltpu.VMEM((rows, d), bf16),
            pltpu.VMEM((rows, wl), bf16),
            pltpu.VMEM((rows, wl), f32),
            pltpu.VMEM((layers, HALVES, half, wl), f32),
            pltpu.VMEM((layers, HALVES, half, wl), f32),
            pltpu.VMEM((layers, HALVES, half, wl), bf16),
            pltpu.VMEM((layers, HALVES, half, wl), bf16),
            dma((6 + layers,)),
            dma((layers, HALVES, n)),
            dma((layers, HALVES, n)),
            dma((layers, HALVES, n)),
            dma((layers, HALVES, n)),
            dma((layers, HALVES)),
            dma((layers, HALVES)),
            dma((layers, HALVES)),
            dma((layers, HALVES)),
            dma,
            dma,
        ],
        compiler_params=pltpu.CompilerParams(
            collective_id=1, has_side_effects=True, vmem_limit_bytes=60 * 1024 * 1024
        ),
    )(
        candidates,
        w_in.reshape(layers, d, 4, wl // LANES, LANES)
        .transpose(0, 1, 3, 2, 4)
        .reshape(layers, wide, LANES),
        key_cache,
        value_cache,
        w_out,
        rab_table.transpose(0, 2, 1),
        hist_bucket.reshape(1, hist_dev),
        hist_len,
        visible,
    )


def in_pairs(mesh):
    n = mesh.shape["hist"]
    if n != 8:
        return False
    index = [slice(None) if name == "hist" else 0 for name in mesh.axis_names]
    spots = [getattr(device, "coords", None) for device in mesh.devices[tuple(index)][:3]]
    if any(spot is None for spot in spots):
        return False
    apart = [sum(abs(a - b) for a, b in zip(spots[0], spot)) for spot in spots[1:]]
    return apart == [1, 1]


def solution(mesh):
    placed = (
        P(("users", "hist"), None),
        P(None, ("users", "hist"), "head"),
        P(None, ("users", "hist"), "head"),
        P(None, None, None, "head"),
        P(None, "head", None),
        P(None, None, "head"),
        P(("users", "hist")),
        P(("users", "hist")),
        P(None, ("users", "hist")),
    )
    chosen = pair_shards if in_pairs(mesh) else shards
    return jax.shard_map(
        functools.partial(chosen, mesh.shape["hist"]),
        mesh=mesh,
        in_specs=placed,
        out_specs=P(("users", "hist"), None),
        check_vma=False,
    )
```

```python
import functools

import jax
import jax.numpy as jnp
from jax import lax
from jax.experimental import pallas as pl
from jax.experimental.pallas import tpu as pltpu
from jax.sharding import PartitionSpec as P

DH = 64
BLOCK = 256
LANES = 128
PER = LANES // DH
GROUP_ROWS = 256
KEY_CHUNK = 2048
BIG = 16384.0
MESH = pl.DeviceIdType.MESH
HALVES = 2
SENDS = ((3, 0), (3, 1), (0, 1), (1, 0), (1, 1))
GATHER = ((3, 0), (3, 1), (1, 0), (1, 1), (2, 0), (2, 1), (0, 1))
ORDER = ((1, 3, 0, 2, 2, 1, 3, 0), (1, 3, 0, 2, 1, 3, 0, 2))
ORDERS = [sum(dz << (2 * t) for t, dz in enumerate(order)) for order in ORDER]
FORWARD = (2, 3)
SUM_A = (7, 7)
SUM_B = 0
END_B = 0

epsilon = 1e-05


def silu(v):
    return v / (1.0 + jnp.exp(-v))


def dot(a, b):
    return jnp.dot(a, b, preferred_element_type=jnp.float32)


def kernel(
    n,
    cand_hbm,
    w_hbm,
    key_hbm,
    val_hbm,
    wo_hbm,
    rab_hbm,
    bucket_hbm,
    hlen,
    vis,
    out,
    cand,
    raw,
    wide,
    w_in,
    w_out,
    rab,
    bucket,
    keys,
    vals,
    kaug,
    table,
    events,
    w_other,
    qall,
    qaug,
    part,
    parts_in,
    acc,
    att_send,
    att_in,
    gate_send,
    gate_in,
    load_sem,
    q_send,
    q_recv,
    p_send,
    p_recv,
    h_send,
    h_recv,
):
    me = lax.axis_index("hist")
    other = 1 - lax.axis_index("head")
    layers, hist_dev, wl = key_hbm.shape
    rows, d = cand.shape
    heads = wl // DH
    parts_w = 4
    pairs = wl // LANES
    nb = rab.shape[2]
    micro, blocks = vis.shape
    total = n * rows
    micro_rows = total // micro
    group_rows = min(GROUP_ROWS, total)
    per_group = group_rows // rows
    groups = n // per_group
    key_chunk = min(KEY_CHUNK, hist_dev)

    load_k = pltpu.make_async_copy(key_hbm, keys, load_sem.at[0])
    load_v = pltpu.make_async_copy(val_hbm, vals, load_sem.at[1])
    load_c = pltpu.make_async_copy(cand_hbm, cand, load_sem.at[2])
    load_w = [
        pltpu.make_async_copy(w_hbm.at[l], raw.at[l], load_sem.at[3 + l]) for l in range(layers)
    ]
    load_o = pltpu.make_async_copy(wo_hbm, w_out, load_sem.at[3 + layers])
    load_r = pltpu.make_async_copy(rab_hbm, rab, load_sem.at[4 + layers])
    load_b = pltpu.make_async_copy(bucket_hbm, bucket, load_sem.at[5 + layers])
    load_c.start()
    load_w[0].start()
    load_b.start()
    load_r.start()
    load_k.start()
    load_o.start()
    load_v.start()
    for copy in load_w[1:]:
        copy.start()

    barrier = pltpu.get_barrier_semaphore()
    for j in range(1, n):
        pl.semaphore_signal(
            barrier, inc=1, device_id={"hist": lax.rem(me + j, n)}, device_id_type=MESH
        )
    pl.semaphore_signal(barrier, inc=1, device_id={"head": other}, device_id_type=MESH)

    def to_head(src, dst, index):
        return pltpu.make_async_remote_copy(
            src_ref=src,
            dst_ref=dst,
            send_sem=h_send.at[index],
            recv_sem=h_recv.at[index],
            device_id={"head": other},
            device_id_type=MESH,
        )

    def unpack_w(l):
        halves = wl // LANES
        step = halves * parts_w
        wide[...] = raw[l].astype(jnp.float32)
        for i in range(parts_w):
            for c in range(halves):
                start = i * wl + c * LANES
                w_in[:, start : start + LANES] = wide[
                    pl.ds(c * parts_w + i, d, stride=step), :
                ].astype(jnp.bfloat16)

    def row_of(s):
        return pl.ds(pl.multiple_of(s * rows, rows), rows)

    def q_copy(l, s, owner):
        return pltpu.make_async_remote_copy(
            src_ref=qall.at[l, row_of(owner)],
            dst_ref=qall.at[l, row_of(owner)],
            send_sem=q_send.at[l, s],
            recv_sem=q_recv.at[l, owner],
            device_id={"hist": s},
            device_id_type=MESH,
        )

    def p_copy(l, s, owner):
        return pltpu.make_async_remote_copy(
            src_ref=part.at[l, row_of(s)],
            dst_ref=parts_in.at[l, owner],
            send_sem=p_send.at[l, s],
            recv_sem=p_recv.at[l, owner],
            device_id={"hist": s},
            device_id_type=MESH,
        )

    def build_keys():
        lane = lax.broadcasted_iota(jnp.int32, (LANES, LANES), 1)
        lane8 = lax.broadcasted_iota(jnp.int32, (blocks, LANES), 1)
        row8 = lax.broadcasted_iota(jnp.int32, (blocks, LANES), 0)
        base_of = (DH, 0)
        seen = []
        gone = []
        for base in base_of:
            held = jnp.zeros((blocks, LANES), jnp.float32)
            for m in range(micro):
                column = jnp.zeros((blocks, LANES), jnp.float32)
                for b in range(blocks):
                    value = (vis[m, b] - 1).astype(jnp.float32) * BIG
                    column = jnp.where(row8 == b, value, column)
                held = jnp.where(lane8 == base + 2 + m, column, held)
            seen.append(held)
            is_micro = (lane8 >= base + 2) & (lane8 < base + 2 + micro)
            gone.append(jnp.where(is_micro & (row8 == 0), -BIG, 0.0))
        for l in range(layers):
            flat = jnp.concatenate([rab[l], jnp.zeros((heads, LANES - nb), jnp.float32)], axis=1)
            flat = jnp.concatenate([flat, jnp.zeros((8 - heads, LANES), jnp.float32)], axis=0)
            upright = flat.T
            for h in range(heads):
                base = base_of[h % PER]
                half = upright[:nb, h : h + 1] * 0.5
                high = half.astype(jnp.bfloat16).astype(jnp.float32)
                low = half - high
                lane_nb = lane[:nb]
                bias = jnp.where(lane_nb == base, high, jnp.where(lane_nb == base + 1, low, 0.0))
                fill = jnp.zeros((LANES - nb - 2 * blocks, LANES), jnp.float32)
                whole = jnp.concatenate([bias, seen[h % PER], gone[h % PER], fill], axis=0)
                start = (l * heads + h) * LANES
                table[:, start : start + LANES] = whole.astype(jnp.bfloat16)

        row = lax.broadcasted_iota(jnp.int32, (LANES, key_chunk), 0)
        spot = lax.broadcasted_iota(jnp.int32, (LANES, key_chunk), 1)
        lane_k = lax.broadcasted_iota(jnp.int32, (key_chunk, LANES), 1)
        length = hlen[0]
        for c in range(hist_dev // key_chunk):
            span = slice(c * key_chunk, (c + 1) * key_chunk)
            place = spot + c * key_chunk
            here = (
                (row == bucket[:, span])
                | (row == nb + place // BLOCK)
                | ((row == nb + blocks) & (place >= length))
            )
            events[span, :] = jnp.where(here, 1.0, 0.0).T.astype(jnp.bfloat16)
        load_k.wait()

        def chunk(c, carry):
            span = pl.ds(pl.multiple_of(c * key_chunk, key_chunk), key_chunk)
            spread = events[span, :]
            for l in range(layers):
                for h in range(heads):
                    start = (l * heads + h) * LANES
                    extra = dot(spread, table[:, start : start + LANES])
                    p = h // PER
                    tile = keys[l, span, p * LANES : (p + 1) * LANES].astype(jnp.float32)
                    mine = (lane_k < DH) if h % PER == 0 else (lane_k >= DH)
                    kaug[l, h, span, :] = jnp.where(mine, tile, extra).astype(jnp.bfloat16)
            return carry

        lax.fori_loop(0, hist_dev // key_chunk, chunk, 0)

    lane_q = lax.broadcasted_iota(jnp.int32, (group_rows, LANES), 1)
    row_q = lax.broadcasted_iota(jnp.int32, (group_rows, LANES), 0)
    lane_a = lax.broadcasted_iota(jnp.int32, (group_rows, LANES), 1)

    def attend(l, g):
        span = pl.ds(pl.multiple_of(g * group_rows, group_rows), group_rows)
        which = (row_q + g * group_rows) // micro_rows
        for h in range(heads):
            p = h // PER
            base = DH if h % PER == 0 else 0
            tile = qall[l, span, p * LANES : (p + 1) * LANES].astype(jnp.float32)
            ones = (lane_q == base) | (lane_q == base + 1) | (lane_q == base + 2 + which)
            mine = (lane_q < DH) if h % PER == 0 else (lane_q >= DH)
            qaug[h] = jnp.where(mine, tile, jnp.where(ones, 1.0, 0.0)).astype(jnp.bfloat16)
        acc[...] = jnp.zeros_like(acc)

        def chunk(c, carry):
            keys_at = pl.ds(pl.multiple_of(c * key_chunk, key_chunk), key_chunk)
            for p in range(pairs):
                value = vals[l, keys_at, p * LANES : (p + 1) * LANES]
                found = []
                for e in range(PER):
                    h = p * PER + e
                    y = lax.dot_general(
                        qaug[h],
                        kaug[l, h, keys_at, :],
                        (((1,), (1,)), ((), ())),
                        preferred_element_type=jnp.float32,
                    ).astype(jnp.bfloat16)
                    weight = y * (jnp.tanh(y) + 1.0)
                    found.append(dot(weight, value))
                acc[:, p * LANES : (p + 1) * LANES] += jnp.where(lane_a < DH, found[0], found[1])
            return carry

        lax.fori_loop(0, hist_dev // key_chunk, chunk, 0)
        part[l, span, :] = acc[...].astype(jnp.bfloat16)

    block_row = lax.broadcasted_iota(jnp.int32, (wl, wl), 0) // DH
    block_col = lax.broadcasted_iota(jnp.int32, (wl, wl), 1) // DH
    same_head = jnp.where(block_row == block_col, 1.0, 0.0).astype(jnp.bfloat16)

    load_c.wait()
    stream = cand[...].astype(jnp.float32)
    for l in range(layers):
        load_w[l].wait()
        unpack_w(l)
        average = jnp.mean(stream, axis=-1, keepdims=True)
        centred = stream - average
        variance = jnp.mean(centred * centred, axis=-1, keepdims=True)
        normed = (centred * lax.rsqrt(variance + epsilon)).astype(jnp.bfloat16)

        def project(i):
            return silu(dot(normed, w_in[:, i * wl : (i + 1) * wl])).astype(jnp.bfloat16)

        queries = project(0).astype(jnp.float32)
        qall[l, row_of(me), :] = (queries * (0.5 * DH**-0.5)).astype(jnp.bfloat16)
        if l == 0:
            pl.semaphore_wait(barrier, n)
        for j in range(1, n):
            q_copy(l, lax.rem(me + j, n), me).start()
        keys_new = project(1).astype(jnp.float32)
        values_new = project(2).astype(jnp.float32)
        gates = project(3)
        gate_send[l] = gates
        gate_copy = to_head(gate_send.at[l], gate_in.at[l], 2 * l)
        gate_copy.start()
        if l == 0:
            load_o.wait()
            w_copy = to_head(w_out, w_other, 2 * layers)
            w_copy.start()
        product = queries * keys_new
        high = product.astype(jnp.bfloat16)
        low = (product - high.astype(jnp.float32)).astype(jnp.bfloat16)
        own_score = dot(high, same_head) + dot(low, same_head)
        own = silu(own_score * (DH**-0.5)) * values_new
        if l == 0:
            load_r.wait()
            load_b.wait()
            build_keys()
            load_v.wait()

        def group(t, carry):
            g = lax.rem(me // per_group + t, groups)
            for i in range(per_group):
                s = g * per_group + i

                @pl.when(s != me)
                def _():
                    q_copy(l, s, s).wait_recv()

            attend(l, g)
            for i in range(per_group):
                s = g * per_group + i

                @pl.when(s != me)
                def _():
                    p_copy(l, s, me).start()

            return carry

        lax.fori_loop(0, groups, group, 0)
        history = part[l, row_of(me), :].astype(jnp.float32)
        for j in range(1, n):
            s = lax.rem(me + j, n)
            p_copy(l, s, s).wait_recv()
            history = history + parts_in[l, s].astype(jnp.float32)
        attended = history + own
        att_send[l] = attended
        att_copy = to_head(att_send.at[l], att_in.at[l], 2 * l + 1)
        att_copy.start()
        if l == 0:
            w_copy.wait_recv()
        gate_copy.wait_recv()
        att_copy.wait_recv()
        theirs = att_in[l]
        width = 2 * wl
        mean = (
            jnp.sum(attended, axis=-1, keepdims=True) + jnp.sum(theirs, axis=-1, keepdims=True)
        ) / width
        square = (
            jnp.sum(attended * attended, axis=-1, keepdims=True)
            + jnp.sum(theirs * theirs, axis=-1, keepdims=True)
        ) / width
        rstd = lax.rsqrt(square - mean * mean + epsilon)
        gated = ((attended - mean) * rstd * gates.astype(jnp.float32)).astype(jnp.bfloat16)
        gated_other = ((theirs - mean) * rstd * gate_in[l].astype(jnp.float32)).astype(
            jnp.bfloat16
        )
        stream = stream + (dot(gated, w_out[l]) + dot(gated_other, w_other[l]))
        gate_copy.wait_send()
        att_copy.wait_send()
        if l == 0:
            w_copy.wait_send()
        for j in range(1, n):
            s = lax.rem(me + j, n)
            q_copy(l, s, me).wait_send()
            p_copy(l, s, me).wait_send()
    out[...] = stream.astype(out.dtype)


def shards(
    n, candidates, key_cache, value_cache, w_in, w_out, rab_table, hist_len, hist_bucket, visible
):
    layers, hist_dev, wl = key_cache.shape
    rows, d = candidates.shape
    heads = wl // DH
    total = n * rows
    group_rows = min(GROUP_ROWS, total)
    bf16, f32 = jnp.bfloat16, jnp.float32
    vmem = pl.BlockSpec(memory_space=pltpu.VMEM)
    smem = pl.BlockSpec(memory_space=pltpu.SMEM)
    hbm = pl.BlockSpec(memory_space=pltpu.HBM)
    dma = pltpu.SemaphoreType.DMA
    return pl.pallas_call(
        functools.partial(kernel, n),
        out_shape=jax.ShapeDtypeStruct((rows, d), bf16),
        in_specs=[hbm, hbm, hbm, hbm, hbm, hbm, hbm, smem, smem],
        out_specs=vmem,
        scratch_shapes=[
            pltpu.VMEM((rows, d), bf16),
            pltpu.VMEM((layers, d * 4 * wl // LANES, LANES), bf16),
            pltpu.VMEM((d * 4 * wl // LANES, LANES), f32),
            pltpu.VMEM((d, 4 * wl), bf16),
            pltpu.VMEM(w_out.shape, bf16),
            pltpu.VMEM((layers, heads, rab_table.shape[1]), f32),
            pltpu.VMEM((1, hist_dev), jnp.int32),
            pltpu.VMEM((layers, hist_dev, wl), bf16),
            pltpu.VMEM((layers, hist_dev, wl), bf16),
            pltpu.VMEM((layers, heads, hist_dev, LANES), bf16),
            pltpu.VMEM((LANES, layers * heads * LANES), bf16),
            pltpu.VMEM((hist_dev, LANES), bf16),
            pltpu.VMEM(w_out.shape, bf16),
            pltpu.VMEM((layers, total, wl), bf16),
            pltpu.VMEM((heads, group_rows, LANES), bf16),
            pltpu.VMEM((layers, total, wl), bf16),
            pltpu.VMEM((layers, n, rows, wl), bf16),
            pltpu.VMEM((group_rows, wl), f32),
            pltpu.VMEM((layers, rows, wl), f32),
            pltpu.VMEM((layers, rows, wl), f32),
            pltpu.VMEM((layers, rows, wl), bf16),
            pltpu.VMEM((layers, rows, wl), bf16),
            dma((6 + layers,)),
            dma((layers, n)),
            dma((layers, n)),
            dma((layers, n)),
            dma((layers, n)),
            dma((2 * layers + 1,)),
            dma((2 * layers + 1,)),
        ],
        compiler_params=pltpu.CompilerParams(
            collective_id=0, has_side_effects=True, vmem_limit_bytes=60 * 1024 * 1024
        ),
    )(
        candidates,
        w_in.reshape(layers, d, 4, wl // LANES, LANES)
        .transpose(0, 1, 3, 2, 4)
        .reshape(layers, d * 4 * wl // LANES, LANES),
        key_cache,
        value_cache,
        w_out,
        rab_table.transpose(0, 2, 1),
        hist_bucket.reshape(1, hist_dev),
        hist_len,
        visible,
    )


def pair_kernel(
    n,
    cand_hbm,
    w_hbm,
    key_hbm,
    val_hbm,
    wo_hbm,
    rab_hbm,
    bucket_hbm,
    hlen,
    vis,
    out,
    cand,
    raw,
    wide,
    w_in,
    w_out,
    rab,
    bucket,
    keys,
    vals,
    kaug,
    table,
    events,
    w_other,
    qall,
    qaug,
    part,
    parts_in,
    stream,
    normed,
    q_own,
    own,
    att_send,
    att_in,
    gate_send,
    gate_in,
    load_sem,
    q_send,
    q_recv,
    p_send,
    p_recv,
    a_send,
    a_recv,
    g_send,
    g_recv,
    w_send,
    w_recv,
):
    me = lax.axis_index("hist")
    other = 1 - lax.axis_index("head")
    layers, hist_dev, wl = key_hbm.shape
    rows, d = cand.shape
    heads = wl // DH
    pairs = wl // LANES
    nb = rab.shape[2]
    micro, blocks = vis.shape
    micro_rows = n * rows // micro
    half = rows // HALVES
    pair = 2 * half
    outer = n // 2
    calls = HALVES * outer
    line, side = me // 2, lax.rem(me, 2)
    beside = line * 2 + 1 - side

    barrier = pltpu.get_barrier_semaphore()
    for j in range(1, n):
        pl.semaphore_signal(
            barrier, inc=1, device_id={"hist": lax.rem(me + j, n)}, device_id_type=MESH
        )
    pl.semaphore_signal(barrier, inc=1, device_id={"head": other}, device_id_type=MESH)

    load_c = pltpu.make_async_copy(cand_hbm, cand, load_sem.at[0])
    load_w = [
        pltpu.make_async_copy(w_hbm.at[l], raw.at[l], load_sem.at[6 + l]) for l in range(layers)
    ]
    load_k = pltpu.make_async_copy(key_hbm, keys, load_sem.at[1])
    load_v = pltpu.make_async_copy(val_hbm, vals, load_sem.at[2])
    load_o = pltpu.make_async_copy(wo_hbm, w_out, load_sem.at[3])
    load_r = pltpu.make_async_copy(rab_hbm, rab, load_sem.at[4])
    load_b = pltpu.make_async_copy(bucket_hbm, bucket, load_sem.at[5])
    load_c.start()
    load_w[0].start()

    load_b.start()
    load_r.start()
    load_k.start()
    load_o.start()
    load_v.start()
    for copy in load_w[1:]:
        copy.start()

    def to_head(src, dst, send, recv):
        return pltpu.make_async_remote_copy(
            src_ref=src,
            dst_ref=dst,
            send_sem=send,
            recv_sem=recv,
            device_id={"head": other},
            device_id_type=MESH,
        )

    w_copy = to_head(w_out, w_other, w_send, w_recv)

    def att_copy(l, f):
        return to_head(att_send.at[l, f], att_in.at[l, f], a_send.at[l, f], a_recv.at[l, f])

    def gate_copy(l, f):
        return to_head(gate_send.at[l, f], gate_in.at[l, f], g_send.at[l, f], g_recv.at[l, f])

    def unit(s):
        return pl.ds(pl.multiple_of(s * half, half), half)

    def unit_pair(z):
        return pl.ds(pl.multiple_of(z * pair, pair), pair)

    def near(dz, dy):
        return lax.rem(line + dz, outer) * 2 + lax.rem(side + dy, 2)

    def q_copy(l, f, s, owner):
        return pltpu.make_async_remote_copy(
            src_ref=qall.at[l, f, unit(owner)],
            dst_ref=qall.at[l, f, unit(owner)],
            send_sem=q_send.at[l, f, s],
            recv_sem=q_recv.at[l, f, owner],
            device_id={"hist": s},
            device_id_type=MESH,
        )

    def relay_copy(l, f, z):
        return pltpu.make_async_remote_copy(
            src_ref=qall.at[l, f, unit_pair(z)],
            dst_ref=qall.at[l, f, unit_pair(z)],
            send_sem=q_send.at[l, f, me],
            recv_sem=q_recv.at[l, f, 2 * z],
            device_id={"hist": near(outer - 1, 0)},
            device_id_type=MESH,
        )

    def p_copy(l, f, s, owner):
        return pltpu.make_async_remote_copy(
            src_ref=part.at[l, f, unit(s)],
            dst_ref=parts_in.at[l, f, owner],
            send_sem=p_send.at[l, f, s],
            recv_sem=p_recv.at[l, f, owner],
            device_id={"hist": s},
            device_id_type=MESH,
        )

    def send_q(l, f):
        for dz, dy in SENDS:
            q_copy(l, f, near(dz, dy), me).start()

    def unpack_w(l, first, last):
        halves = wl // LANES
        step = halves * 4
        if first == 0:
            load_w[l].wait()
            wide[...] = raw[l].astype(jnp.float32)
        for i in range(first, last):
            for c in range(halves):
                start = i * wl + c * LANES
                w_in[l, :, start : start + LANES] = wide[
                    pl.ds(c * 4 + i, d, stride=step), :
                ].astype(jnp.bfloat16)

    def build_tables():
        lane8 = lax.broadcasted_iota(jnp.int32, (blocks, LANES), 1)
        row8 = lax.broadcasted_iota(jnp.int32, (blocks, LANES), 0)
        lane_nb = lax.broadcasted_iota(jnp.int32, (nb, LANES), 1)
        base_of = (DH, 0)
        seen = []
        gone = []
        for base in base_of:
            held = jnp.zeros((blocks, LANES), jnp.float32)
            for m in range(micro):
                column = jnp.zeros((blocks, LANES), jnp.float32)
                for b in range(blocks):
                    value = (vis[m, b] - 1).astype(jnp.float32) * BIG
                    column = jnp.where(row8 == b, value, column)
                held = jnp.where(lane8 == base + 2 + m, column, held)
            seen.append(held)
            is_micro = (lane8 >= base + 2) & (lane8 < base + 2 + micro)
            gone.append(jnp.where(is_micro & (row8 == 0), -BIG, 0.0))
        load_r.wait()
        for l in range(layers):
            flat = jnp.concatenate([rab[l], jnp.zeros((heads, LANES - nb), jnp.float32)], axis=1)
            flat = jnp.concatenate([flat, jnp.zeros((8 - heads, LANES), jnp.float32)], axis=0)
            upright = flat.T
            for h in range(heads):
                base = base_of[h % PER]
                score = upright[:nb, h : h + 1] * 0.5
                high = score.astype(jnp.bfloat16).astype(jnp.float32)
                low = score - high
                bias = jnp.where(lane_nb == base, high, jnp.where(lane_nb == base + 1, low, 0.0))
                fill = jnp.zeros((LANES - nb - 2 * blocks, LANES), jnp.float32)
                whole = jnp.concatenate([bias, seen[h % PER], gone[h % PER], fill], axis=0)
                start = (l * heads + h) * LANES
                table[:, start : start + LANES] = whole.astype(jnp.bfloat16)

        row = lax.broadcasted_iota(jnp.int32, (LANES, hist_dev), 0)
        place = lax.broadcasted_iota(jnp.int32, (LANES, hist_dev), 1)
        load_b.wait()
        here = (
            (row == bucket[...])
            | (row == nb + place // BLOCK)
            | ((row == nb + blocks) & (place >= hlen[0]))
        )
        events[...] = jnp.where(here, 1.0, 0.0).T.astype(jnp.bfloat16)

    def augment_keys(l):
        lane_k = lax.broadcasted_iota(jnp.int32, (hist_dev, LANES), 1)
        for h in range(heads):
            start = (l * heads + h) * LANES
            extra = dot(events[...], table[:, start : start + LANES])
            p = h // PER
            tile = keys[l, :, p * LANES : (p + 1) * LANES].astype(jnp.float32)
            mine = (lane_k < DH) if h % PER == 0 else (lane_k >= DH)
            kaug[l, h] = jnp.where(mine, tile, extra).astype(jnp.bfloat16)

    lane_q = lax.broadcasted_iota(jnp.int32, (pair, LANES), 1)
    row_q = lax.broadcasted_iota(jnp.int32, (pair, LANES), 0)

    def attend(l, f, z):
        span = unit_pair(z)
        place = (z * 2 + row_q // half) * rows + f * half + row_q % half
        which = place // micro_rows
        for h in range(heads):
            p = h // PER
            base = DH if h % PER == 0 else 0
            tile = qall[l, f, span, p * LANES : (p + 1) * LANES].astype(jnp.float32)
            ones = (lane_q == base) | (lane_q == base + 1) | (lane_q == base + 2 + which)
            mine = (lane_q < DH) if h % PER == 0 else (lane_q >= DH)
            qaug[h] = jnp.where(mine, tile, jnp.where(ones, 1.0, 0.0)).astype(jnp.bfloat16)
        for p in range(pairs):
            value = vals[l, :, p * LANES : (p + 1) * LANES]
            found = []
            for e in range(PER):
                h = p * PER + e
                y = lax.dot_general(
                    qaug[h],
                    kaug[l, h],
                    (((1,), (1,)), ((), ())),
                    preferred_element_type=jnp.float32,
                ).astype(jnp.bfloat16)
                weight = y * (jnp.tanh(y) + 1.0)
                found.append(dot(weight, value))
            both = jnp.where(lane_q < DH, found[0], found[1])
            part[l, f, span, p * LANES : (p + 1) * LANES] = both.astype(jnp.bfloat16)

    block_row = lax.broadcasted_iota(jnp.int32, (wl, wl), 0) // DH
    block_col = lax.broadcasted_iota(jnp.int32, (wl, wl), 1) // DH
    same_head = jnp.where(block_row == block_col, 1.0, 0.0).astype(jnp.bfloat16)

    def normalize(l, first, last):
        mine = slice(first * half, last * half)
        x = stream[mine]
        centred = x - jnp.mean(x, axis=-1, keepdims=True)
        variance = jnp.mean(centred * centred, axis=-1, keepdims=True)
        normed[mine] = (centred * lax.rsqrt(variance + epsilon)).astype(jnp.bfloat16)

    def make_queries(l, first, last):
        mine = slice(first * half, last * half)
        queries = silu(dot(normed[mine], w_in[l, :, :wl])).astype(jnp.bfloat16)
        scaled = (queries.astype(jnp.float32) * (0.5 * DH**-0.5)).astype(jnp.bfloat16)
        for f in range(first, last):
            qall[l, f, unit(me)] = scaled[(f - first) * half : (f - first + 1) * half]
        q_own[mine] = queries

    def make_rest(l, first, last):
        mine = slice(first * half, last * half)

        def project(i):
            sums = dot(normed[mine], w_in[l, :, i * wl : (i + 1) * wl])
            return silu(sums).astype(jnp.bfloat16)

        gates = project(3)
        for f in range(first, last):
            gate_send[l, f] = gates[(f - first) * half : (f - first + 1) * half]
            gate_copy(l, f).start()
        keys_new = project(1).astype(jnp.float32)
        values_new = project(2).astype(jnp.float32)
        product = q_own[mine].astype(jnp.float32) * keys_new
        high = product.astype(jnp.bfloat16)
        low = (product - high.astype(jnp.float32)).astype(jnp.bfloat16)
        own_score = dot(high, same_head) + dot(low, same_head)
        own[mine] = silu(own_score * (DH**-0.5)) * values_new

    def add_parts(l, f):
        history = part[l, f, unit(me), :].astype(jnp.float32)
        for dz, dy in GATHER:
            s = near(dz, dy)
            p_copy(l, f, s, s).wait_recv()
            history = history + parts_in[l, f, s].astype(jnp.float32)
        history = history + own[f * half : (f + 1) * half]
        att_send[l, f] = history.astype(jnp.bfloat16)
        att_copy(l, f).start()

    def finish(l, f):
        mine = slice(f * half, (f + 1) * half)
        if l == 0 and f == 0:
            w_copy.wait_recv()
        gate_copy(l, f).wait_recv()
        att_copy(l, f).wait_recv()
        attended = att_send[l, f].astype(jnp.float32)
        theirs = att_in[l, f].astype(jnp.float32)
        width = 2 * wl
        mean = (
            jnp.sum(attended, axis=-1, keepdims=True) + jnp.sum(theirs, axis=-1, keepdims=True)
        ) / width
        square = (
            jnp.sum(attended * attended, axis=-1, keepdims=True)
            + jnp.sum(theirs * theirs, axis=-1, keepdims=True)
        ) / width
        rstd = lax.rsqrt(square - mean * mean + epsilon)
        gates, gates_other = gate_send[l, f], gate_in[l, f]
        gated = ((attended - mean) * rstd * gates.astype(jnp.float32)).astype(jnp.bfloat16)
        gated_other = ((theirs - mean) * rstd * gates_other.astype(jnp.float32)).astype(
            jnp.bfloat16
        )
        x = stream[mine] + (dot(gated, w_out[l]) + dot(gated_other, w_other[l]))
        if l + 1 < layers:
            stream[mine] = x
        else:
            out[mine] = x.astype(out.dtype)

    load_c.wait()
    stream[...] = cand[...].astype(jnp.float32)
    normalize(0, 0, HALVES)
    unpack_w(0, 0, 1)
    make_queries(0, 0, HALVES)

    def prepare():
        build_tables()
        load_k.wait()
        augment_keys(0)
        for l in range(1, layers):
            unpack_w(l, 0, 4)

    pl.semaphore_wait(barrier, n)
    for f in range(HALVES):
        send_q(0, f)
    unpack_w(0, 1, 4)
    make_rest(0, 0, HALVES)
    load_o.wait()
    w_copy.start()
    prepare()
    load_v.wait()

    def call(t, carry):
        l, f = t // calls, (t // outer) % HALVES
        for late in range(layers):
            first = late * calls

            if SUM_A[min(late, 1)] < calls:

                @pl.when(t == first + SUM_A[min(late, 1)])
                def _(late=late):
                    add_parts(late, 0)

            if late + 1 < layers:

                @pl.when(t == first + calls)
                def _(late=late):
                    if SUM_A[min(late, 1)] == calls:
                        add_parts(late, 0)
                    finish(late, 0)
                    normalize(late + 1, 0, 1)
                    make_queries(late + 1, 0, 1)
                    send_q(late + 1, 0)
                    make_rest(late + 1, 0, 1)
                    augment_keys(late + 1)

                @pl.when(t == first + calls + SUM_B)
                def _(late=late):
                    add_parts(late, 1)

                @pl.when(t == first + calls + END_B)
                def _(late=late):
                    finish(late, 1)
                    normalize(late + 1, 1, 2)
                    make_queries(late + 1, 1, 2)
                    send_q(late + 1, 1)
                    make_rest(late + 1, 1, 2)

        kind = jnp.minimum(l, 1)
        code = ORDERS[0] + kind * (ORDERS[1] - ORDERS[0])
        dz = lax.shift_right_logical(code, 2 * (t % calls)) & 3
        z = lax.rem(line + dz, outer)
        @pl.when(dz == 0)
        def _():
            q_copy(l, f, beside, beside).wait_recv()

        @pl.when(t % calls == FORWARD[0] + kind * (FORWARD[1] - FORWARD[0]))
        def _():
            after = lax.rem(line + 1, outer)
            for i in range(2):
                q_copy(l, 1, 2 * after + i, 2 * after + i).wait_recv()
            relay_copy(l, 1, after).start()

        @pl.when(dz == 2)
        def _():
            relay_copy(l, f, z).wait_recv()

        @pl.when((dz == 3) | ((dz == 1) & (f == 0)))
        def _():
            for i in range(2):
                q_copy(l, f, 2 * z + i, 2 * z + i).wait_recv()

        @pl.when((dz == 1) & (f == 0))
        def _():
            relay_copy(l, f, z).start()

        attend(l, f, z)
        for i in range(2):
            s = 2 * z + i

            @pl.when(s != me)
            def _(s=s):
                p_copy(l, f, s, me).start()

        return carry

    lax.fori_loop(0, layers * calls, call, 0)
    if SUM_A[min(layers - 1, 1)] == calls:
        add_parts(layers - 1, 0)
    finish(layers - 1, 0)
    add_parts(layers - 1, 1)
    finish(layers - 1, 1)

    w_copy.wait_send()
    for l in range(layers):
        for f in range(HALVES):
            att_copy(l, f).wait_send()
            gate_copy(l, f).wait_send()
            for dz, dy in SENDS:
                q_copy(l, f, near(dz, dy), me).wait_send()
            relay_copy(l, f, lax.rem(line + 1, outer)).wait_send()
            for j in range(1, n):
                p_copy(l, f, lax.rem(me + j, n), me).wait_send()


def pair_shards(
    n, candidates, key_cache, value_cache, w_in, w_out, rab_table, hist_len, hist_bucket, visible
):
    layers, hist_dev, wl = key_cache.shape
    rows, d = candidates.shape
    heads = wl // DH
    half = rows // HALVES
    bf16, f32 = jnp.bfloat16, jnp.float32
    vmem = pl.BlockSpec(memory_space=pltpu.VMEM)
    smem = pl.BlockSpec(memory_space=pltpu.SMEM)
    hbm = pl.BlockSpec(memory_space=pltpu.HBM)
    dma = pltpu.SemaphoreType.DMA
    wide = d * 4 * wl // LANES
    return pl.pallas_call(
        functools.partial(pair_kernel, n),
        out_shape=jax.ShapeDtypeStruct((rows, d), bf16),
        in_specs=[hbm, hbm, hbm, hbm, hbm, hbm, hbm, smem, smem],
        out_specs=vmem,
        scratch_shapes=[
            pltpu.VMEM((rows, d), bf16),
            pltpu.VMEM((layers, wide, LANES), bf16),
            pltpu.VMEM((wide, LANES), f32),
            pltpu.VMEM((layers, d, 4 * wl), bf16),
            pltpu.VMEM(w_out.shape, bf16),
            pltpu.VMEM((layers, heads, rab_table.shape[1]), f32),
            pltpu.VMEM((1, hist_dev), jnp.int32),
            pltpu.VMEM((layers, hist_dev, wl), bf16),
            pltpu.VMEM((layers, hist_dev, wl), bf16),
            pltpu.VMEM((layers, heads, hist_dev, LANES), bf16),
            pltpu.VMEM((LANES, layers * heads * LANES), bf16),
            pltpu.VMEM((hist_dev, LANES), bf16),
            pltpu.VMEM(w_out.shape, bf16),
            pltpu.VMEM((layers, HALVES, n * half, wl), bf16),
            pltpu.VMEM((heads, 2 * half, LANES), bf16),
            pltpu.VMEM((layers, HALVES, n * half, wl), bf16),
            pltpu.VMEM((layers, HALVES, n, half, wl), bf16),
            pltpu.VMEM((rows, d), f32),
            pltpu.VMEM((rows, d), bf16),
            pltpu.VMEM((rows, wl), bf16),
            pltpu.VMEM((rows, wl), f32),
            pltpu.VMEM((layers, HALVES, half, wl), bf16),
            pltpu.VMEM((layers, HALVES, half, wl), bf16),
            pltpu.VMEM((layers, HALVES, half, wl), bf16),
            pltpu.VMEM((layers, HALVES, half, wl), bf16),
            dma((6 + layers,)),
            dma((layers, HALVES, n)),
            dma((layers, HALVES, n)),
            dma((layers, HALVES, n)),
            dma((layers, HALVES, n)),
            dma((layers, HALVES)),
            dma((layers, HALVES)),
            dma((layers, HALVES)),
            dma((layers, HALVES)),
            dma,
            dma,
        ],
        compiler_params=pltpu.CompilerParams(
            collective_id=1, has_side_effects=True, vmem_limit_bytes=60 * 1024 * 1024
        ),
    )(
        candidates,
        w_in.reshape(layers, d, 4, wl // LANES, LANES)
        .transpose(0, 1, 3, 2, 4)
        .reshape(layers, wide, LANES),
        key_cache,
        value_cache,
        w_out,
        rab_table.transpose(0, 2, 1),
        hist_bucket.reshape(1, hist_dev),
        hist_len,
        visible,
    )


def in_pairs(mesh):
    n = mesh.shape["hist"]
    if n != 8:
        return False
    index = [slice(None) if name == "hist" else 0 for name in mesh.axis_names]
    spots = [getattr(device, "coords", None) for device in mesh.devices[tuple(index)][:3]]
    if any(spot is None for spot in spots):
        return False
    apart = [sum(abs(a - b) for a, b in zip(spots[0], spot)) for spot in spots[1:]]
    return apart == [1, 1]


def solution(mesh):
    placed = (
        P(("users", "hist"), None),
        P(None, ("users", "hist"), "head"),
        P(None, ("users", "hist"), "head"),
        P(None, None, None, "head"),
        P(None, "head", None),
        P(None, None, "head"),
        P(("users", "hist")),
        P(("users", "hist")),
        P(None, ("users", "hist")),
    )
    chosen = pair_shards if in_pairs(mesh) else shards
    return jax.shard_map(
        functools.partial(chosen, mesh.shape["hist"]),
        mesh=mesh,
        in_specs=placed,
        out_specs=P(("users", "hist"), None),
        check_vma=False,
    )
```
